512 devices in a mesh: dom: 128 (over z, y, x_lo), serve: 4 (over x_hi, core).
Axes of the slice: x: 4 (x_hi: 2, x_lo: 2; x = x_hi * 2 + x_lo), y: 4, z: 16, core: 2. Of those that a mesh axis runs over, the one named last changes fastest.
Arguments:
- source_rows: float32 [128, 4, 256, 400], P('dom', 'serve'), may hold values from -1.5 to 1.5
- source_state: float32 [128, 4, 256], P('dom', 'serve'), may hold values from 0.01 to 1
- target_rows: float32 [128, 4, 256, 400], P('dom', 'serve'), may hold values from -1.5 to 1.5
- target_state: float32 [128, 4, 256], P('dom', 'serve'), may hold values from 0.01 to 1
- relation_table: float32 [16, 400], replicated, may hold values from -4 to 4
- source_ids: int32 [128, 4, 2, 8, 128], P('dom', 'serve'), may hold values from 0 to 255
- target_ids: int32 [128, 4, 2, 8, 128], P('dom', 'serve'), may hold values from 0 to 255
- relation_ids: int32 [128, 4, 2, 8, 128], P('dom', 'serve'), may hold values from 0 to 15
- negative_block: int32 [128, 4, 2, 8], P('dom', 'serve'), may hold values from 0 to 1
- edge_counts: int32 [128, 4, 2, 8], P('dom', 'serve'), may hold values from 1 to 128, 768 in all within a row
- serving_shard: int32 [128, 4, 256], P('dom', 'serve'), may hold values from 0 to 3
- changed_rows: int32 [128, 4, 256], P('dom', 'serve'), may hold values from 0 to 1, as said below
Outputs:
- new_source: float32 [128, 4, 256, 400], P('dom', 'serve')
- new_source_state: float32 [128, 4, 256], P('dom', 'serve')
- new_target: float32 [128, 4, 256, 400], P('dom', 'serve')
- new_target_state: float32 [128, 4, 256], P('dom', 'serve')
- served: bfloat16 [128, 4, 4, 256, 400], P('dom', 'serve')
The draws below stay inside these ranges and needn't reach their ends.
Inputs may be any that keep to these rules, and one draw needn't show every extreme that they name: `edge_counts`: for one device and step, the 8 counts sum to 768 and the largest is exactly 128. `changed_rows`: on every device at most 64 changed rows have one serving shard, and exactly 64 have some shard, the same shard for all devices of one index of dom.
All inputs are finite; a program needn't handle non-finite values.
Results may differ from the reference program's by a relative error of at most 0.001.
Values may be sent and summed in bfloat16 or wider, within the bound.
No kernel may reach another device: no remote copies, remote signals or barrier semaphores. Data moves between devices by JAX's collectives and lax.ppermute only.
A program may use at most 64 MiB of HBM per device.

```python
import math
import jax
import jax.numpy as jnp
import numpy as np
from jax import lax

D = 400
NREL = 16
EDGE_BLOCK = 128
STEPS = 2
ROWS = 256
NB = 8
PARTITIONS = 128
SHARDS = 4


def serving_plan(key):
    base = jax.random.fold_in(key, 7)
    perm_key, order_key, count_key = jax.random.split(base, 3)
    devices_count = PARTITIONS * SHARDS
    row_perms = jax.vmap(lambda single: jax.random.permutation(single, ROWS))(jax.random.split(perm_key, devices_count))
    position = jnp.argsort(row_perms, axis=1).astype(jnp.int32)
    segment = (position >= ROWS // 2).astype(jnp.int32) + (position >= 3 * ROWS // 4).astype(jnp.int32) + (position >= 7 * ROWS // 8).astype(jnp.int32)
    starts = jnp.array([0, ROWS // 2, 3 * ROWS // 4, 7 * ROWS // 8], jnp.int32)
    orders = jax.vmap(lambda single: jax.random.permutation(single, 4))(jax.random.split(order_key, PARTITIONS)).astype(jnp.int32)
    orders = jnp.repeat(orders, SHARDS, axis=0)
    shard_of_row = jnp.take_along_axis(orders, segment, axis=1)
    upper = jnp.array([ROWS // 4, ROWS // 8, ROWS // 8], jnp.int32)
    others = jax.random.randint(count_key, (devices_count, 3), 1, upper[None, :] + 1).astype(jnp.int32)
    limits = jnp.concatenate([jnp.full((devices_count, 1), ROWS // 4, jnp.int32), others], axis=1)
    offset = position - starts[segment]
    chosen = (offset < jnp.take_along_axis(limits, segment, axis=1)).astype(jnp.int32)
    return (shard_of_row.reshape(PARTITIONS, SHARDS, ROWS), chosen.reshape(PARTITIONS, SHARDS, ROWS))


def draw_serving_shard(key, part):
    return serving_plan(key)[0]


def draw_changed_rows(key, part):
    return serving_plan(key)[1]


def place_ends(values, stream_key, low, largest):
    extent = values.shape
    place = [jax.random.randint(jax.random.fold_in(stream_key, axis), (), 0, extent[axis]) for axis in range(len(extent))]
    values = values.at[tuple(place)].set(low)
    longest = extent.index(max(extent))
    place[longest] = (place[longest] + 1) % extent[longest]
    return values.at[tuple(place)].set(largest)


def steps_of(key, extent, cuts, smallest, high):
    def one(axis_at, shards_of):
        heights = jax.random.uniform(jax.random.fold_in(jax.random.fold_in(key, 6), axis_at), (shards_of,), jnp.float32, smallest / len(cuts), high / len(cuts))
        return jnp.repeat(jnp.exp(heights), extent[axis_at] // shards_of).reshape((-1,) + (1,) * (len(extent) - axis_at - 1))

    level = one(*cuts[0])
    for cut in cuts[1:]:
        level = level * one(*cut)
    return level


def split_up(number_of, total, bound, lean):
    loads = [(1 << 20) // math.isqrt(rank ** lean) + 1 for rank in range(2, number_of + 1)]
    surplus, given = total - bound - (number_of - 1), [1] * (number_of - 1)
    while surplus > 0:
        free = [i for i in range(number_of - 1) if given[i] < bound]
        whole, remaining = sum([loads[i] for i in free]), surplus
        for i in free:
            extra = min(bound - given[i], max(1, remaining * loads[i] // whole), surplus)
            given[i] = given[i] + extra
            surplus = surplus - extra
    return np.array([bound] + given)


def uneven_parts(stream_key, number_of, total, reach, skew):
    if number_of == 2:
        one = jax.random.randint(stream_key, (), max(1, total - reach), min(reach, total - 1) + 1)
        return jnp.stack([one, total - one])
    lengths = jnp.asarray(split_up(number_of, total, reach, skew), jnp.int32)
    twos = (number_of - 1) // 2
    giver, taker = lengths[1:1 + 2 * twos:2], lengths[2:2 + 2 * twos:2]
    slack = jnp.minimum(giver - 1, reach - taker)
    moved = jax.random.randint(jax.random.fold_in(stream_key, 1), (twos,), 0, 1 << 20) % (slack + 1)
    lengths = lengths.at[1:1 + 2 * twos:2].set(giver - moved).at[2:2 + 2 * twos:2].set(taker + moved)
    return lengths[jax.random.permutation(jax.random.fold_in(stream_key, 2), number_of)]


def noise(stream_key, extent, deviation, most, cuts=(), kind=jnp.bfloat16):
    values = deviation * jax.random.normal(stream_key, extent, jnp.float32)
    if cuts:
        values = values * steps_of(stream_key, extent, cuts, -0.22, 0.18)
    return jnp.clip(values, -most, most).astype(kind)


def setup_inputs(seed: int = 0) -> dict:
    seeds = jax.random.split(jax.random.key(seed), 13)
    source_rows = noise(seeds[0], (PARTITIONS, SHARDS, ROWS, D), 0.25, 1.5, ((0, 128), (1, 4)), jnp.float32)
    source_state = jnp.clip(jnp.exp(math.log(1.0) - 4.6051702 * jax.random.uniform(seeds[1], (PARTITIONS, SHARDS, ROWS), jnp.float32) ** steps_of(seeds[1], (PARTITIONS, SHARDS, ROWS), ((0, 128), (1, 4)), -0.2, 0.2)), 0.01, 1.0)
    target_rows = noise(seeds[2], (PARTITIONS, SHARDS, ROWS, D), 0.25, 1.5, ((0, 128), (1, 4)), jnp.float32)
    target_state = jnp.clip(jnp.exp(math.log(1.0) - 4.6051702 * jax.random.uniform(seeds[3], (PARTITIONS, SHARDS, ROWS), jnp.float32) ** steps_of(seeds[3], (PARTITIONS, SHARDS, ROWS), ((0, 128), (1, 4)), -0.2, 0.2)), 0.01, 1.0)
    relation_table = noise(seeds[4], (NREL, D), 1.0, 4.0, (), jnp.float32)
    source_ids = place_ends(jax.random.randint(seeds[5], (PARTITIONS, SHARDS, STEPS, NB, EDGE_BLOCK), 0, ROWS), jax.random.fold_in(seeds[5], 1), 0, ROWS - 1).astype(jnp.int32)
    target_ids = place_ends(jax.random.randint(seeds[6], (PARTITIONS, SHARDS, STEPS, NB, EDGE_BLOCK), 0, ROWS), jax.random.fold_in(seeds[6], 1), 0, ROWS - 1).astype(jnp.int32)
    relation_ids = place_ends(jax.random.randint(seeds[7], (PARTITIONS, SHARDS, STEPS, NB, EDGE_BLOCK), 0, NREL), jax.random.fold_in(seeds[7], 1), 0, NREL - 1).astype(jnp.int32)
    negative_block = place_ends(jax.random.randint(seeds[8], (PARTITIONS, SHARDS, STEPS, NB), 0, ROWS // 128), jax.random.fold_in(seeds[8], 1), 0, (ROWS // 128) - 1).astype(jnp.int32)
    edge_counts = jax.vmap(lambda own: uneven_parts(own, NB, 96 * NB, EDGE_BLOCK, 2))(jax.random.split(seeds[9], PARTITIONS * SHARDS * STEPS)).reshape((PARTITIONS, SHARDS, STEPS, NB)).astype(jnp.int32)
    serving_shard = draw_serving_shard(jax.random.fold_in(seeds[12], 71), 0)
    changed_rows = draw_changed_rows(jax.random.fold_in(seeds[12], 71), 0)
    return dict(source_rows=source_rows, source_state=source_state, target_rows=target_rows, target_state=target_state, relation_table=relation_table, source_ids=source_ids, target_ids=target_ids, relation_ids=relation_ids, negative_block=negative_block, edge_counts=edge_counts, serving_shard=serving_shard, changed_rows=changed_rows)


HIGHEST_PRECISION = lax.Precision.HIGHEST
LEARN_RATE = 0.1
EPSILON = 1e-08

def adagrad_update(weights, state, gradient):
    new_state = state + lax.optimization_barrier(jnp.mean(gradient * gradient, axis=-1))
    return (weights - LEARN_RATE * gradient / (jnp.sqrt(new_state)[:, None] + EPSILON), new_state)

def train_bucket(source, source_sums, target, target_sums, edge_source, edge_target, edge_relation, negative_ids, counts, relation_table):
    blocks, lanes_count = edge_source.shape
    row_count, width = source.shape
    relation_count = relation_table.shape[0]
    per_group = min(8, blocks)
    lane_ids = jnp.arange(lanes_count, dtype=jnp.int32)
    grad_source = jnp.zeros((row_count, width), source.dtype)
    grad_target = jnp.zeros((row_count, width), source.dtype)
    for block_start in range(0, blocks, per_group):
        source_idx = edge_source[block_start:block_start + per_group]
        target_idx = edge_target[block_start:block_start + per_group]
        relation_idx = edge_relation[block_start:block_start + per_group]
        negative_idx = negative_ids[block_start:block_start + per_group][:, None] * lanes_count + lane_ids[None, :]
        source_part = source[source_idx]
        target_part = target[target_idx]
        negative_part = target[negative_idx]
        selector = (relation_idx.reshape(-1)[:, None] == jnp.arange(relation_count, dtype=jnp.int32)[None, :]).astype(source.dtype)
        relation_part = jnp.dot(selector, relation_table, precision=HIGHEST_PRECISION).reshape(per_group, lanes_count, width)
        query = source_part * relation_part
        positive = lax.optimization_barrier(jnp.sum(query * target_part, axis=-1))
        negative = jnp.einsum('gid,gjd->gij', query, negative_part, precision=HIGHEST_PRECISION)
        valid = (lane_ids[None, :] < counts[block_start:block_start + per_group][:, None]).astype(source.dtype)
        positive_grad = -jax.nn.sigmoid(-positive) * valid
        negative_grad = jax.nn.sigmoid(negative) * (valid[:, :, None] / lanes_count)
        query_grad = positive_grad[..., None] * target_part + jnp.einsum('gij,gjd->gid', negative_grad, negative_part, precision=HIGHEST_PRECISION)
        grad_source = grad_source.at[source_idx.reshape(-1)].add((query_grad * relation_part).reshape(-1, width))
        grad_target = grad_target.at[target_idx.reshape(-1)].add((positive_grad[..., None] * query).reshape(-1, width))
        negative_term = jnp.einsum('gij,gid->gjd', negative_grad, query, precision=HIGHEST_PRECISION)
        grad_target = grad_target.at[negative_idx.reshape(-1)].add(negative_term.reshape(-1, width))
    source, source_sums = adagrad_update(source, source_sums, grad_source)
    target, target_sums = adagrad_update(target, target_sums, grad_target)
    return (source, source_sums, target, target_sums)

def reference(source_rows, source_state, target_rows, target_state, relation_table, source_ids, target_ids, relation_ids, negative_block, edge_counts, serving_shard, changed_rows):
    parts, shards, row_count, width = source_rows.shape

    def flatten(array):
        return array.reshape((parts * shards,) + array.shape[2:])

    def unflatten(array):
        return array.reshape((parts, shards) + array.shape[1:])
    source, source_sums = (source_rows, source_state)
    target, target_sums = (target_rows, target_state)
    for bucket in range(STEPS):
        target = jnp.roll(target, 1, axis=0)
        target_sums = jnp.roll(target_sums, 1, axis=0)

        def per_device(packed):
            return train_bucket(*packed, relation_table)
        results = lax.map(per_device, (flatten(source), flatten(source_sums), flatten(target), flatten(target_sums), flatten(source_ids[:, :, bucket]), flatten(target_ids[:, :, bucket]), flatten(relation_ids[:, :, bucket]), flatten(negative_block[:, :, bucket]), flatten(edge_counts[:, :, bucket])))
        source, source_sums, target, target_sums = [unflatten(item) for item in results]
    published = source.astype(jnp.bfloat16)
    nothing = jnp.zeros((), jnp.bfloat16)
    pieces = []
    for shard in range(shards):
        keep = (serving_shard == shard) & (changed_rows == 1)
        pieces.append(jnp.where(keep[..., None], published, nothing))
    served = jnp.stack(pieces, axis=1)
    return (source, source_sums, target, target_sums, served)
```

```python
import jax
import jax.numpy as jnp
from jax import lax
from jax.experimental import pallas as pl
from jax.experimental.pallas import tpu as pltpu
from jax.sharding import PartitionSpec as P

LEARN_RATE = 0.1
EPSILON = 1e-08
SLOTS = 64

F32 = jnp.float32
BF16 = jnp.bfloat16
NN = ((1,), (0,))
NT = ((1,), (1,))
TN = ((0,), (0,))
LANES = 128
CHUNK = 2


def dot(a, b, dims):
    return lax.dot_general(a, b, (dims, ((), ())), preferred_element_type=F32)


def halves(x):
    high = x.astype(BF16)
    return high, (x - high.astype(F32)).astype(BF16)


def sigmoid(x):
    return 0.5 + 0.5 * jnp.tanh(0.5 * x)


def one_hot(ids, rows):
    place = lax.broadcasted_iota(jnp.int32, (rows, ids.shape[1]), 0)
    return (place == ids).astype(F32).astype(BF16)


def row_of(ids_ref, step, first):
    return jnp.concatenate([ids_ref[step, b : b + 1, :] for b in range(first, first + CHUNK)], axis=1)


def make_queries(step, source, relation3, src_ref, rel_ref, q_high, q_low, rel_out):
    high, low = halves(source)
    stacked = jnp.concatenate([high, low], axis=0)
    width = source.shape[0]
    nrel = relation3.shape[0] // 3
    for first in range(0, src_ref.shape[1], CHUNK):
        at = pl.ds(first * LANES, CHUNK * LANES)
        both = dot(stacked, one_hot(row_of(src_ref, step, first), source.shape[1]), NN)
        pick = one_hot(row_of(rel_ref, step, first), nrel)
        relation = dot(relation3, jnp.concatenate([pick, pick, pick], axis=0), TN)
        query = (both[:width] + both[width:]) * relation
        qh, ql = halves(query)
        q_high[:, at] = qh
        q_low[:, at] = ql
        rel_out[:, at] = relation


def relation_parts(relation):
    high = relation.astype(BF16)
    rest = relation - high.astype(F32)
    middle = rest.astype(BF16)
    low = (rest - middle.astype(F32)).astype(BF16)
    return jnp.concatenate([high, middle, low], axis=0)


def score_gradients(step, first, target_parts, q_high, q_low, tgt_ref, nb_ref, count_ref):
    rows = target_parts.shape[1] // 2
    at = pl.ds(first * LANES, CHUNK * LANES)
    qh = q_high[:, at]
    ql = q_low[:, at]
    both = dot(target_parts, qh, TN)
    scores = both[:rows] + both[rows:] + dot(target_parts[:, :rows], ql, TN)
    pieces = []
    lane = lax.broadcasted_iota(jnp.int32, (1, LANES), 1)
    place = lax.broadcasted_iota(jnp.int32, (rows, LANES), 0)
    for b in range(CHUNK):
        sc = scores[:, b * LANES : (b + 1) * LANES]
        hit = place == tgt_ref[step, first + b : first + b + 1, :]
        valid = (lane < count_ref[step, first + b]).astype(F32)
        positive = jnp.sum(jnp.where(hit, sc, 0.0), axis=0, keepdims=True)
        dpos = -sigmoid(-positive) * valid
        upper = nb_ref[step, first + b] == 0
        negative = jnp.where(upper, sc[:LANES], sc[LANES:])
        dneg = sigmoid(negative) * (valid * (1.0 / LANES))
        spread = jnp.concatenate([jnp.where(upper, dneg, 0.0), jnp.where(upper, 0.0, dneg)], axis=0)
        pieces.append(spread + jnp.where(hit, dpos, 0.0))
    return halves(jnp.concatenate(pieces, axis=1))


def adagrad(weights, state, gradient):
    new_state = state + jnp.sum(gradient * gradient, axis=0, keepdims=True) * (1.0 / gradient.shape[0])
    scale = LEARN_RATE / (jnp.sqrt(new_state) + EPSILON)
    return weights - gradient * scale, new_state


def target_gradient(qh, ql, gh, gl):
    width = qh.shape[0]
    both = dot(jnp.concatenate([qh, ql], axis=0), gh, NT)
    return both[:width] + both[width:] + dot(qh, gl, NT)


def source_gradient(step, first, target_stack, gh, gl, rel, src_ref):
    width = rel.shape[0]
    both = dot(target_stack, gh, NN)
    flow = (both[:width] + both[width:] + dot(target_stack[:width], gl, NN)) * rel
    fh, fl = halves(flow)
    rows = one_hot(row_of(src_ref, step, first), gh.shape[0])
    both = dot(jnp.concatenate([fh, fl], axis=0), rows, NT)
    return both[:width] + both[width:]


def prepare_kernel(source, relation, src_ref, rel_ref, q_high, q_low, rel_out):
    make_queries(0, source[...], relation_parts(relation[...]), src_ref, rel_ref, q_high, q_low, rel_out)


def target_kernel(target, state, q_high, q_low, tgt_ref, nb_ref, count_ref, new_target, new_state, g_high, g_low):
    high, low = halves(target[...])
    parts = jnp.concatenate([high, low], axis=1)
    gradient = jnp.zeros(target.shape, F32)
    for first in range(0, tgt_ref.shape[1], CHUNK):
        at = pl.ds(first * LANES, CHUNK * LANES)
        gh, gl = score_gradients(0, first, parts, q_high, q_low, tgt_ref, nb_ref, count_ref)
        g_high[:, at] = gh
        g_low[:, at] = gl
        gradient += target_gradient(q_high[:, at], q_low[:, at], gh, gl)
    new_target[...], new_state[...] = adagrad(target[...], state[...], gradient)


def source_kernel(target, source, state, relation, g_high, g_low, rel_in, src_ref, rel_ref,
                  new_source, new_state, q_high, q_low, rel_out):
    high, low = halves(target[...])
    stack = jnp.concatenate([high, low], axis=0)
    gradient = jnp.zeros(source.shape, F32)
    for first in range(0, src_ref.shape[1], CHUNK):
        at = pl.ds(first * LANES, CHUNK * LANES)
        gradient += source_gradient(0, first, stack, g_high[:, at], g_low[:, at], rel_in[:, at], src_ref)
    updated, sums = adagrad(source[...], state[...], gradient)
    new_source[...] = updated
    new_state[...] = sums
    make_queries(1, updated, relation_parts(relation[...]), src_ref, rel_ref, q_high, q_low, rel_out)


def publish(updated, shard, changed, outgoing):
    width, rows = updated.shape
    half = width // 2
    is_row = lax.broadcasted_iota(jnp.int32, (8, rows), 0)
    mine = jnp.logical_and(is_row == shard, changed == 1).astype(F32)
    before = (lax.broadcasted_iota(jnp.int32, (rows, rows), 0) < lax.broadcasted_iota(jnp.int32, (rows, rows), 1))
    rank = dot(mine.astype(BF16), before.astype(F32).astype(BF16), NN)
    slot = jnp.sum(mine * rank, axis=0, keepdims=True).astype(jnp.int32)
    code = jnp.where(changed == 1, shard * (2 * SLOTS) + slot, -1)
    shards = outgoing.shape[0]
    place = lax.broadcasted_iota(jnp.int32, (shards * 2 * SLOTS, rows), 0)
    top = (place == code).astype(F32).astype(BF16)
    bottom = jnp.logical_and(place == code + SLOTS, code >= 0).astype(F32).astype(BF16)
    number = (lax.broadcasted_iota(jnp.int32, (8, rows), 1) + 1).astype(F32)
    packed = dot(jnp.concatenate([updated[:half], number], axis=0).astype(BF16), top, NT)
    packed += dot(jnp.concatenate([updated[half:], number], axis=0).astype(BF16), bottom, NT)
    for s in range(shards):
        outgoing[s] = packed[:, s * 2 * SLOTS : (s + 1) * 2 * SLOTS].astype(BF16)


def last_source_kernel(target, source, state, q_high, q_low, rel_in, src_ref, tgt_ref, nb_ref, count_ref, shard, changed,
                       new_source, new_state, g_high, g_low, outgoing):
    high, low = halves(target[...])
    parts = jnp.concatenate([high, low], axis=1)
    stack = jnp.concatenate([high, low], axis=0)
    gradient = jnp.zeros(source.shape, F32)
    for first in range(0, src_ref.shape[1], CHUNK):
        at = pl.ds(first * LANES, CHUNK * LANES)
        gh, gl = score_gradients(1, first, parts, q_high, q_low, tgt_ref, nb_ref, count_ref)
        g_high[:, at] = gh
        g_low[:, at] = gl
        gradient += source_gradient(1, first, stack, gh, gl, rel_in[:, at], src_ref)
    updated, sums = adagrad(source[...], state[...], gradient)
    new_source[...] = updated
    new_state[...] = sums
    publish(updated, shard[...], changed[...], outgoing)


def last_target_kernel(target, state, q_high, q_low, g_high, g_low, new_target, new_state):
    gradient = jnp.zeros(target.shape, F32)
    step = CHUNK * LANES
    for first in range(0, q_high.shape[1], step):
        at = pl.ds(first, step)
        gradient += target_gradient(q_high[:, at], q_low[:, at], g_high[:, at], g_low[:, at])
    new_target[...], new_state[...] = adagrad(target[...], state[...], gradient)


def serve_kernel(incoming, served):
    shards, packed_rows, lanes = incoming.shape
    half = served.shape[1] // 2
    rows = served.shape[2]
    lane = lax.broadcasted_iota(jnp.int32, (rows, lanes), 1)
    number = (lax.broadcasted_iota(jnp.int32, (rows, lanes), 0) + 1).astype(F32)
    for s in range(shards):
        block = incoming[s]
        index = block[half : half + 8].astype(F32)[:1]
        match = number == index
        top = jnp.logical_and(match, lane < SLOTS).astype(F32)
        bottom = jnp.logical_and(match, lane >= SLOTS).astype(F32)
        spread = dot(block, jnp.concatenate([top, bottom], axis=0).astype(BF16), NT)
        served[s] = jnp.concatenate([spread[:half, :rows], spread[:half, rows:]], axis=0).astype(BF16)


VMEM = pl.BlockSpec(memory_space=pltpu.VMEM)
SMEM = pl.BlockSpec(memory_space=pltpu.SMEM)


def call(kernel, outs, args, scalars=(), flops=10**9):
    return pl.pallas_call(
        kernel,
        out_shape=[jax.ShapeDtypeStruct(shape, kind) for shape, kind in outs],
        in_specs=[SMEM if i in scalars else VMEM for i in range(len(args))],
        out_specs=[VMEM] * len(outs),
        compiler_params=pltpu.CompilerParams(vmem_limit_bytes=40 * 2**20),
        cost_estimate=pl.CostEstimate(flops=flops, bytes_accessed=4 * 2**20, transcendentals=2**17),
    )(*args)


def from_behind(block, axis, distance):
    devices = range(lax.axis_size(axis))
    route = [((i - distance) % len(devices), i) for i in devices]
    return lax.ppermute(block, axis, route)


def on_device(
    source_rows,
    source_state,
    target_rows,
    target_state,
    relation_table,
    source_ids,
    target_ids,
    relation_ids,
    negative_block,
    edge_counts,
    serving_shard,
    changed_rows,
):
    source = jnp.swapaxes(source_rows[0, 0], 0, 1)
    target = jnp.swapaxes(target_rows[0, 0], 0, 1)
    source_sums, target_sums = source_state[0], target_state[0]
    src, tgt, rel = source_ids[0, 0], target_ids[0, 0], relation_ids[0, 0]
    negatives, counts = negative_block[0, 0], edge_counts[0, 0]
    width, rows = source.shape
    edges = src.shape[1] * src.shape[2]
    shards = lax.axis_size("serve")
    matrix, line = ((width, rows), F32), ((1, rows), F32)
    edge16, edge32, grad16 = ((width, edges), BF16), ((width, edges), F32), ((rows, edges), BF16)

    target = from_behind(target, "dom", 1)
    target_sums = from_behind(target_sums, "dom", 1)
    q_high, q_low, relation = call(prepare_kernel, [edge16, edge16, edge32], (source, relation_table, src, rel))
    moved, moved_sums, g_high, g_low = call(
        target_kernel, [matrix, line, grad16, grad16],
        (target, target_sums, q_high, q_low, tgt, negatives, counts), (5, 6))
    moved = from_behind(moved, "dom", 1)
    moved_sums = from_behind(moved_sums, "dom", 1)
    source, source_sums, q_high, q_low, relation = call(
        source_kernel, [matrix, line, edge16, edge16, edge32],
        (target, source, source_sums, relation_table, g_high, g_low, relation, src, rel))
    target, target_sums = moved, moved_sums
    source, source_sums, g_high, g_low, outgoing = call(
        last_source_kernel, [matrix, line, grad16, grad16, ((shards, width // 2 + 8, 2 * SLOTS), BF16)],
        (target, source, source_sums, q_high, q_low, relation, src, tgt, negatives, counts, serving_shard[0], changed_rows[0]),
        (8, 9))
    incoming = lax.all_to_all(outgoing, "serve", split_axis=0, concat_axis=0, tiled=True)
    target, target_sums = call(last_target_kernel, [matrix, line], (target, target_sums, q_high, q_low, g_high, g_low))
    served = call(serve_kernel, [((shards, width, rows), BF16)], (incoming,))[0]
    return (
        jnp.swapaxes(source, 0, 1)[None, None],
        source_sums[None],
        jnp.swapaxes(target, 0, 1)[None, None],
        target_sums[None],
        jnp.swapaxes(served, 1, 2)[None, None],
    )


def solution(mesh):
    return jax.shard_map(
        on_device,
        mesh=mesh,
        in_specs=(
            P("dom", "serve", None, None),
            P("dom", "serve", None),
            P("dom", "serve", None, None),
            P("dom", "serve", None),
            P(),
            P("dom", "serve", None, None, None),
            P("dom", "serve", None, None, None),
            P("dom", "serve", None, None, None),
            P("dom", "serve", None, None),
            P("dom", "serve", None, None),
            P("dom", "serve", None),
            P("dom", "serve", None),
        ),
        out_specs=(
            P("dom", "serve", None, None),
            P("dom", "serve", None),
            P("dom", "serve", None, None),
            P("dom", "serve", None),
            P("dom", "serve", None, None, None),
        ),
        check_vma=False,
    )
```

```python
import jax
import jax.numpy as jnp
from jax import lax
from jax.experimental import pallas as pl
from jax.experimental.pallas import tpu as pltpu
from jax.sharding import PartitionSpec as P

LEARN_RATE = 0.1
EPSILON = 1e-08
SLOTS = 64

F32 = jnp.float32
BF16 = jnp.bfloat16
NN = ((1,), (0,))
NT = ((1,), (1,))
TN = ((0,), (0,))
LANES = 128
CHUNK = 256
LIVE = 768
SCALE_UNIT = 16384.0
CODE_MAX = 32767.0
TAIL = 16


def dot(a, b, dims):
    return lax.dot_general(a, b, (dims, ((), ())), preferred_element_type=F32)


def halves(x):
    high = x.astype(BF16)
    return high, (x - high.astype(F32)).astype(BF16)


def sigmoid(x):
    return 0.5 + 0.5 * jnp.tanh(0.5 * x)


def one_hot(ids, rows):
    place = lax.broadcasted_iota(jnp.int32, (rows, ids.shape[1]), 0)
    return (place == ids).astype(F32).astype(BF16)


def compact(step, src_ref, tgt_ref, rel_ref, nb_ref, count_ref):
    blocks, lanes = src_ref.shape[1:]
    stack = jnp.concatenate([src_ref[step], tgt_ref[step], rel_ref[step], jnp.zeros_like(src_ref[step])], axis=0)
    stack = stack.astype(F32)
    row = lax.broadcasted_iota(jnp.int32, stack.shape, 0)
    edge = lax.broadcasted_iota(jnp.int32, (lanes, LIVE), 0)
    apart = lax.broadcasted_iota(jnp.int32, (lanes, LIVE), 1) - edge
    packed = jnp.zeros((stack.shape[0], LIVE), F32)
    start = 0
    for b in range(blocks):
        count = count_ref[step, b]
        block = nb_ref[step, b].astype(F32)
        mine = jnp.where(row % blocks == b, stack + jnp.where(row >= 3 * blocks, block, 0.0), 0.0)
        to = jnp.logical_and(apart == start, edge < count)
        packed += dot(mine.astype(BF16), to.astype(F32).astype(BF16), NN)
        start = start + count
    return [
        jnp.sum(packed[i * blocks : (i + 1) * blocks], axis=0, keepdims=True).astype(jnp.int32) for i in range(4)
    ]


def pick_rows(rows, values, shape):
    row = lax.broadcasted_iota(jnp.int32, shape, 0)
    out = jnp.zeros(shape, jnp.int32)
    for i, value in zip(rows, values):
        out = jnp.where(row == i, value, out)
    return out


def coded(x):
    largest = jnp.max(jnp.abs(x), axis=0, keepdims=True)
    unit = jnp.floor(largest * SCALE_UNIT) + 1.0
    code = jnp.floor(x * ((CODE_MAX * SCALE_UNIT) / unit) + 0.5)
    return code.astype(jnp.int32), unit.astype(jnp.int32)


def decoded(codes, unit):
    return codes.astype(F32) * (unit.astype(F32) * (1.0 / (CODE_MAX * SCALE_UNIT)))


def relation_parts(relation):
    high = relation.astype(BF16)
    rest = relation - high.astype(F32)
    middle = rest.astype(BF16)
    low = (rest - middle.astype(F32)).astype(BF16)
    return jnp.concatenate([high, middle, low], axis=0)


def queries(source_stack, relation3, src, rel):
    width = source_stack.shape[0] // 2
    relations = relation3.shape[0] // 3
    both = dot(source_stack, one_hot(src, source_stack.shape[1]), NN)
    pick = one_hot(rel, relations)
    relation = dot(relation3, jnp.concatenate([pick, pick, pick], axis=0), TN)
    qh, ql = halves((both[:width] + both[width:]) * relation)
    return qh, ql, relation


def score_gradients(target_parts, qh, ql, tgt, block):
    rows = target_parts.shape[1] // 2
    lanes = tgt.shape[1]
    both = dot(target_parts, qh, TN)
    scores = both[:rows] + both[rows:] + dot(target_parts[:, :rows], ql, TN)
    hit = lax.broadcasted_iota(jnp.int32, (rows, lanes), 0) == tgt
    positive = jnp.sum(jnp.where(hit, scores, 0.0), axis=0, keepdims=True)
    dpos = -sigmoid(-positive)
    upper = jnp.broadcast_to(block, (LANES, lanes)) == 0
    negative = jnp.where(upper, scores[:LANES], scores[LANES:])
    dneg = sigmoid(negative) * (1.0 / LANES)
    spread = jnp.concatenate([jnp.where(upper, dneg, 0.0), jnp.where(upper, 0.0, dneg)], axis=0)
    return halves(spread + jnp.where(hit, dpos, 0.0))


def adagrad(weights, state, gradient):
    new_state = state + jnp.sum(gradient * gradient, axis=0, keepdims=True) * (1.0 / gradient.shape[0])
    scale = LEARN_RATE / (jnp.sqrt(new_state) + EPSILON)
    return weights - gradient * scale, new_state


def target_gradient(qh, ql, gh, gl):
    width = qh.shape[0]
    both = dot(jnp.concatenate([qh, ql], axis=0), gh, NT)
    return both[:width] + both[width:] + dot(qh, gl, NT)


def source_gradient(target_stack, gh, gl, relation, src):
    width = relation.shape[0]
    both = dot(target_stack, gh, NN)
    flow = (both[:width] + both[width:] + dot(target_stack[:width], gl, NN)) * relation
    fh, fl = halves(flow)
    both = dot(jnp.concatenate([fh, fl], axis=0), one_hot(src, gh.shape[0]), NT)
    return both[:width] + both[width:]


def encode_target_kernel(target, state, payload):
    codes, unit = coded(target[...])
    scaled = state[...] * SCALE_UNIT
    whole = jnp.floor(scaled)
    part = jnp.floor((scaled - whole) * SCALE_UNIT + 0.5)
    tail = pick_rows(
        range(3), [unit, whole.astype(jnp.int32), part.astype(jnp.int32)], (TAIL, target.shape[1]))
    payload[...] = jnp.concatenate([codes, tail], axis=0).astype(jnp.int16)


def encode_source_kernel(source, src_ref, tgt_ref, rel_ref, nb_ref, count_ref, payload, ids_now, ids_next):
    codes, unit = coded(source[...])
    rows = source.shape[1]
    ids = compact(0, src_ref, tgt_ref, rel_ref, nb_ref, count_ref)
    ids_now[...] = pick_rows(range(4), ids, ids_now.shape)
    pieces = [i[:, at : at + rows] for i in ids for at in range(0, LIVE, rows)]
    tail = pick_rows(range(TAIL), [unit] + pieces, (TAIL, rows))
    payload[...] = jnp.concatenate([codes, tail], axis=0).astype(jnp.int16)
    ids = compact(1, src_ref, tgt_ref, rel_ref, nb_ref, count_ref)
    ids_next[...] = pick_rows(range(4), ids, ids_next.shape)


def query_kernel(source, relation, ids, q_high, q_low, rel_out):
    stack = jnp.concatenate(halves(source[...]), axis=0)
    relation3 = relation_parts(relation[...])
    for first in range(0, LIVE, CHUNK):
        at = pl.ds(first, CHUNK)
        q_high[:, at], q_low[:, at], rel_out[:, at] = queries(stack, relation3, ids[0:1, at], ids[2:3, at])


def source_kernel(payload, source, state, relation, ids, ids_next, q_high, q_low, rel_in,
                  new_source, new_state, next_high, next_low, next_rel):
    width = source.shape[0]
    packed = payload[...].astype(jnp.int32)
    high, low = halves(decoded(packed[:width], packed[width : width + 1]))
    parts = jnp.concatenate([high, low], axis=1)
    stack = jnp.concatenate([high, low], axis=0)
    gradient = jnp.zeros(source.shape, F32)
    for first in range(0, LIVE, CHUNK):
        at = pl.ds(first, CHUNK)
        gh, gl = score_gradients(parts, q_high[:, at], q_low[:, at], ids[1:2, at], ids[3:4, at])
        gradient += source_gradient(stack, gh, gl, rel_in[:, at], ids[0:1, at])
    updated, sums = adagrad(source[...], state[...], gradient)
    new_source[...] = updated
    new_state[...] = sums
    stack = jnp.concatenate(halves(updated), axis=0)
    relation3 = relation_parts(relation[...])
    for first in range(0, LIVE, CHUNK):
        at = pl.ds(first, CHUNK)
        next_high[:, at], next_low[:, at], next_rel[:, at] = queries(
            stack, relation3, ids_next[0:1, at], ids_next[2:3, at])


def publish(updated, shard, changed, outgoing):
    width, rows = updated.shape
    half = width // 2
    is_row = lax.broadcasted_iota(jnp.int32, (8, rows), 0)
    mine = jnp.logical_and(is_row == shard, changed == 1).astype(F32)
    before = (lax.broadcasted_iota(jnp.int32, (rows, rows), 0) < lax.broadcasted_iota(jnp.int32, (rows, rows), 1))
    rank = dot(mine.astype(BF16), before.astype(F32).astype(BF16), NN)
    slot = jnp.sum(mine * rank, axis=0, keepdims=True).astype(jnp.int32)
    code = jnp.where(changed == 1, shard * (2 * SLOTS) + slot, -1)
    shards = outgoing.shape[0]
    place = lax.broadcasted_iota(jnp.int32, (shards * 2 * SLOTS, rows), 0)
    top = (place == code).astype(F32).astype(BF16)
    bottom = jnp.logical_and(place == code + SLOTS, code >= 0).astype(F32).astype(BF16)
    number = (lax.broadcasted_iota(jnp.int32, (8, rows), 1) + 1).astype(F32)
    packed = dot(jnp.concatenate([updated[:half], number], axis=0).astype(BF16), top, NT)
    packed += dot(jnp.concatenate([updated[half:], number], axis=0).astype(BF16), bottom, NT)
    for s in range(shards):
        outgoing[s] = packed[:, s * 2 * SLOTS : (s + 1) * 2 * SLOTS].astype(BF16)


def main_kernel(target_payload, source_payload, relation, source, state, ids, q_high, q_low, rel_in, shard, changed,
                new_source, new_state, new_target, new_target_state, g_high, g_low, outgoing):
    width, rows = source.shape
    packed = target_payload[...].astype(jnp.int32)
    target = decoded(packed[:width], packed[width : width + 1])
    tail = packed[width : width + TAIL].astype(F32)
    target_state = (tail[1:2] + tail[2:3] * (1.0 / SCALE_UNIT)) * (1.0 / SCALE_UNIT)
    packed = source_payload[...].astype(jnp.int32)
    tail = packed[width : width + TAIL]
    behind = jnp.concatenate(halves(decoded(packed[:width], tail[0:1])), axis=0)
    relation3 = relation_parts(relation[...])
    parts = jnp.concatenate(halves(target), axis=1)
    gradient = jnp.zeros(source.shape, F32)
    pieces = LIVE // rows
    for i in range(pieces):
        src, tgt, rel, block = [tail[1 + j * pieces + i : 2 + j * pieces + i] for j in range(4)]
        qh, ql, _ = queries(behind, relation3, src, rel)
        gh, gl = score_gradients(parts, qh, ql, tgt, block)
        gradient += target_gradient(qh, ql, gh, gl)
    target, sums = adagrad(target, target_state, gradient)
    new_target[...] = target
    new_target_state[...] = sums
    high, low = halves(target)
    parts = jnp.concatenate([high, low], axis=1)
    stack = jnp.concatenate([high, low], axis=0)
    gradient = jnp.zeros(source.shape, F32)
    for first in range(0, LIVE, CHUNK):
        at = pl.ds(first, CHUNK)
        gh, gl = score_gradients(parts, q_high[:, at], q_low[:, at], ids[1:2, at], ids[3:4, at])
        g_high[:, at] = gh
        g_low[:, at] = gl
        gradient += source_gradient(stack, gh, gl, rel_in[:, at], ids[0:1, at])
    updated, sums = adagrad(source[...], state[...], gradient)
    new_source[...] = updated
    new_state[...] = sums
    publish(updated, shard[...], changed[...], outgoing)


def last_target_kernel(target, state, q_high, q_low, g_high, g_low, new_target, new_state):
    gradient = jnp.zeros(target.shape, F32)
    for first in range(0, LIVE, CHUNK):
        at = pl.ds(first, CHUNK)
        gradient += target_gradient(q_high[:, at], q_low[:, at], g_high[:, at], g_low[:, at])
    new_target[...], new_state[...] = adagrad(target[...], state[...], gradient)


def serve_kernel(incoming, served):
    shards, packed_rows, lanes = incoming.shape
    half = served.shape[1] // 2
    rows = served.shape[2]
    lane = lax.broadcasted_iota(jnp.int32, (rows, lanes), 1)
    number = (lax.broadcasted_iota(jnp.int32, (rows, lanes), 0) + 1).astype(F32)
    for s in range(shards):
        block = incoming[s]
        index = block[half : half + 8].astype(F32)[:1]
        match = number == index
        top = jnp.logical_and(match, lane < SLOTS).astype(F32)
        bottom = jnp.logical_and(match, lane >= SLOTS).astype(F32)
        spread = dot(block, jnp.concatenate([top, bottom], axis=0).astype(BF16), NT)
        served[s] = jnp.concatenate([spread[:half, :rows], spread[:half, rows:]], axis=0).astype(BF16)


VMEM = pl.BlockSpec(memory_space=pltpu.VMEM)
SMEM = pl.BlockSpec(memory_space=pltpu.SMEM)


def call(kernel, outs, args, scalars=(), flops=10**9):
    return pl.pallas_call(
        kernel,
        out_shape=[jax.ShapeDtypeStruct(shape, kind) for shape, kind in outs],
        in_specs=[SMEM if i in scalars else VMEM for i in range(len(args))],
        out_specs=[VMEM] * len(outs),
        compiler_params=pltpu.CompilerParams(vmem_limit_bytes=40 * 2**20),
        cost_estimate=pl.CostEstimate(flops=flops, bytes_accessed=4 * 2**20, transcendentals=2**17),
    )(*args)


def from_behind(block, axis, distance):
    devices = range(lax.axis_size(axis))
    route = [((i - distance) % len(devices), i) for i in devices]
    return lax.ppermute(block, axis, route)


def on_device(
    source_rows,
    source_state,
    target_rows,
    target_state,
    relation_table,
    source_ids,
    target_ids,
    relation_ids,
    negative_block,
    edge_counts,
    serving_shard,
    changed_rows,
):
    source = jnp.swapaxes(source_rows[0, 0], 0, 1)
    target = jnp.swapaxes(target_rows[0, 0], 0, 1)
    source_sums, target_sums = source_state[0], target_state[0]
    src, tgt, rel = source_ids[0, 0], target_ids[0, 0], relation_ids[0, 0]
    negatives, counts = negative_block[0, 0], edge_counts[0, 0]
    width, rows = source.shape
    shards = lax.axis_size("serve")
    matrix, line = ((width, rows), F32), ((1, rows), F32)
    edge16, edge32, grad16 = ((width, LIVE), BF16), ((width, LIVE), F32), ((rows, LIVE), BF16)
    payload, ids8 = ((width + TAIL, rows), jnp.int16), ((8, LIVE), jnp.int32)

    target_out = call(encode_target_kernel, [payload], (target, target_sums))[0]
    near_target = from_behind(target_out, "dom", 1)
    far_target = from_behind(target_out, "dom", 2)
    source_out, ids, ids_next = call(
        encode_source_kernel, [payload, ids8, ids8],
        (source, src, tgt, rel, negatives, counts), (4, 5))
    near_source = from_behind(source_out, "dom", 1)
    q_high, q_low, relation = call(query_kernel, [edge16, edge16, edge32], (source, relation_table, ids))
    source, source_sums, q_high, q_low, relation = call(
        source_kernel, [matrix, line, edge16, edge16, edge32],
        (near_target, source, source_sums, relation_table, ids, ids_next, q_high, q_low, relation))
    source, source_sums, target, target_sums, g_high, g_low, outgoing = call(
        main_kernel, [matrix, line, matrix, line, grad16, grad16, ((shards, width // 2 + 8, 2 * SLOTS), BF16)],
        (far_target, near_source, relation_table, source, source_sums, ids_next, q_high, q_low, relation,
         serving_shard[0], changed_rows[0]))
    incoming = lax.all_to_all(outgoing, "serve", split_axis=0, concat_axis=0, tiled=True)
    target, target_sums = call(last_target_kernel, [matrix, line], (target, target_sums, q_high, q_low, g_high, g_low))
    served = call(serve_kernel, [((shards, width, rows), BF16)], (incoming,))[0]
    return (
        jnp.swapaxes(source, 0, 1)[None, None],
        source_sums[None],
        jnp.swapaxes(target, 0, 1)[None, None],
        target_sums[None],
        jnp.swapaxes(served, 1, 2)[None, None],
    )


def solution(mesh):
    return jax.shard_map(
        on_device,
        mesh=mesh,
        in_specs=(
            P("dom", "serve", None, None),
            P("dom", "serve", None),
            P("dom", "serve", None, None),
            P("dom", "serve", None),
            P(),
            P("dom", "serve", None, None, None),
            P("dom", "serve", None, None, None),
            P("dom", "serve", None, None, None),
            P("dom", "serve", None, None),
            P("dom", "serve", None, None),
            P("dom", "serve", None),
            P("dom", "serve", None),
        ),
        out_specs=(
            P("dom", "serve", None, None),
            P("dom", "serve", None),
            P("dom", "serve", None, None),
            P("dom", "serve", None),
            P("dom", "serve", None, None, None),
        ),
        check_vma=False,
    )
```

```python
import jax
import jax.numpy as jnp
from jax import lax
from jax.experimental import pallas as pl
from jax.experimental.pallas import tpu as pltpu
from jax.sharding import PartitionSpec as P

LEARN_RATE = 0.1
EPSILON = 1e-08
SLOTS = 64

F32 = jnp.float32
BF16 = jnp.bfloat16
NN = ((1,), (0,))
NT = ((1,), (1,))
TN = ((0,), (0,))
LANES = 128
CHUNK = 768
LIVE = 768
SCALE_UNIT = 16384.0
CODE_MAX = 32767.0
TAIL = 16


def dot(a, b, dims):
    return lax.dot_general(a, b, (dims, ((), ())), preferred_element_type=F32)


def halves(x):
    high = x.astype(BF16)
    return high, (x - high.astype(F32)).astype(BF16)


def sigmoid(x):
    return 0.5 + 0.5 * jnp.tanh(0.5 * x)


def one_hot(ids, rows):
    place = lax.broadcasted_iota(jnp.int32, (rows, ids.shape[1]), 0)
    return (place == ids).astype(F32).astype(BF16)


def compact(step, src_ref, tgt_ref, rel_ref, nb_ref, count_ref):
    blocks, lanes = src_ref.shape[1:]
    stack = jnp.concatenate([src_ref[step], tgt_ref[step], rel_ref[step], jnp.zeros_like(src_ref[step])], axis=0)
    stack = stack.astype(F32)
    row = lax.broadcasted_iota(jnp.int32, stack.shape, 0)
    edge = lax.broadcasted_iota(jnp.int32, (lanes, LIVE), 0)
    apart = lax.broadcasted_iota(jnp.int32, (lanes, LIVE), 1) - edge
    packed = jnp.zeros((stack.shape[0], LIVE), F32)
    start = 0
    for b in range(blocks):
        count = count_ref[step, b]
        block = nb_ref[step, b].astype(F32)
        mine = jnp.where(row % blocks == b, stack + jnp.where(row >= 3 * blocks, block, 0.0), 0.0)
        to = jnp.logical_and(apart == start, edge < count)
        packed += dot(mine.astype(BF16), to.astype(F32).astype(BF16), NN)
        start = start + count
    return [
        jnp.sum(packed[i * blocks : (i + 1) * blocks], axis=0, keepdims=True).astype(jnp.int32) for i in range(4)
    ]


def pick_rows(rows, values, shape):
    row = lax.broadcasted_iota(jnp.int32, shape, 0)
    out = jnp.zeros(shape, jnp.int32)
    for i, value in zip(rows, values):
        out = jnp.where(row == i, value, out)
    return out


def coded(x):
    largest = jnp.max(jnp.abs(x), axis=0, keepdims=True)
    unit = jnp.floor(largest * SCALE_UNIT) + 1.0
    code = jnp.floor(x * ((CODE_MAX * SCALE_UNIT) / unit) + 0.5)
    return code.astype(jnp.int32), unit.astype(jnp.int32)


def decoded(codes, unit):
    return codes.astype(F32) * (unit.astype(F32) * (1.0 / (CODE_MAX * SCALE_UNIT)))


def relation_parts(relation):
    high = relation.astype(BF16)
    rest = relation - high.astype(F32)
    middle = rest.astype(BF16)
    low = (rest - middle.astype(F32)).astype(BF16)
    return jnp.concatenate([high, middle, low], axis=0)


def queries(source_stack, relation3, src, rel):
    relations = relation3.shape[0] // 3
    rows = one_hot(src, source_stack.shape[1] // 2)
    pick = one_hot(rel, relations)
    relation = dot(relation3, jnp.concatenate([pick, pick, pick], axis=0), TN)
    qh, ql = halves(dot(source_stack, jnp.concatenate([rows, rows], axis=0), NN) * relation)
    return qh, ql, relation


def score_gradients(target_parts, qh, ql, tgt, block):
    rows = target_parts.shape[0]
    lanes = tgt.shape[1]
    scores = dot(target_parts, jnp.concatenate([qh, qh, ql], axis=0), NN)
    hit = lax.broadcasted_iota(jnp.int32, (rows, lanes), 0) == tgt
    positive = jnp.sum(jnp.where(hit, scores, 0.0), axis=0, keepdims=True)
    dpos = -sigmoid(-positive)
    upper = jnp.broadcast_to(block, (LANES, lanes)) == 0
    negative = jnp.where(upper, scores[:LANES], scores[LANES:])
    dneg = sigmoid(negative) * (1.0 / LANES)
    spread = jnp.concatenate([jnp.where(upper, dneg, 0.0), jnp.where(upper, 0.0, dneg)], axis=0)
    return halves(spread + jnp.where(hit, dpos, 0.0))


def row_major(high, low):
    return jnp.concatenate([high.T, low.T, high.T], axis=1)


def adagrad(weights, state, gradient):
    new_state = state + jnp.sum(gradient * gradient, axis=0, keepdims=True) * (1.0 / gradient.shape[0])
    scale = LEARN_RATE / (jnp.sqrt(new_state) + EPSILON)
    return weights - gradient * scale, new_state


def target_gradient(qh, ql, gh, gl):
    return dot(jnp.concatenate([qh, ql, qh], axis=1), jnp.concatenate([gh, gh, gl], axis=1), NT)


def source_gradient(target_stack, gh, gl, relation, src):
    flow = dot(target_stack, jnp.concatenate([gh, gh, gl], axis=0), NN) * relation
    rows = one_hot(src, gh.shape[0])
    return dot(jnp.concatenate(halves(flow), axis=1), jnp.concatenate([rows, rows], axis=1), NT)


def encode_target_kernel(target, payload):
    codes, unit = coded(target[...])
    tail = pick_rows((0,), [unit], (TAIL, target.shape[1]))
    payload[...] = jnp.concatenate([codes, tail], axis=0).astype(jnp.int16)


def encode_source_kernel(source, src, tgt, rel, nb_ref, count_ref, near, state, payload, far, ids_now):
    width, rows = source.shape
    codes, unit = coded(source[...])
    ids = compact(0, src, tgt, rel, nb_ref, count_ref)
    ids_now[...] = pick_rows(range(4), ids, ids_now.shape)
    pieces = [i[:, at : at + rows] for i in ids for at in range(0, LIVE, rows)]
    tail = pick_rows(range(TAIL), [unit] + pieces, (TAIL, rows))
    payload[...] = jnp.concatenate([codes, tail], axis=0).astype(jnp.int16)
    scaled = state[...] * SCALE_UNIT
    whole = jnp.floor(scaled)
    part = jnp.floor((scaled - whole) * SCALE_UNIT + 0.5)
    unit = near[width : width + TAIL].astype(jnp.int32)[:1]
    tail = pick_rows(range(3), [unit, whole.astype(jnp.int32), part.astype(jnp.int32)], (TAIL, rows))
    far[:width] = near[:width]
    far[width:] = tail.astype(jnp.int16)


def query_kernel(source, relation, ids, src_ref, tgt_ref, rel_ref, nb_ref, count_ref, shard, changed,
                 q_high, q_low, rel_out, ids_next, top, bottom):
    stack = jnp.concatenate(halves(source[...]), axis=1)
    relation3 = relation_parts(relation[...])
    for first in range(0, LIVE, CHUNK):
        at = pl.ds(first, CHUNK)
        q_high[:, at], q_low[:, at], rel_out[:, at] = queries(stack, relation3, ids[0:1, at], ids[2:3, at])
    ids_next[...] = pick_rows(range(4), compact(1, src_ref, tgt_ref, rel_ref, nb_ref, count_ref), ids_next.shape)
    slots(shard[...], changed[...], top, bottom)


def behind_kernel(payload, relation, q_high, q_low, ids):
    width, rows = payload.shape[0] - TAIL, payload.shape[1]
    packed = payload[...].astype(jnp.int32)
    tail = packed[width:]
    stack = jnp.concatenate(halves(decoded(packed[:width], tail[0:1])), axis=1)
    relation3 = relation_parts(relation[...])
    pieces = LIVE // rows
    for i in range(pieces):
        at = pl.ds(i * rows, rows)
        src, tgt, rel, block = [tail[1 + j * pieces + i : 2 + j * pieces + i] for j in range(4)]
        q_high[:, at], q_low[:, at], _ = queries(stack, relation3, src, rel)
        ids[:, at] = pick_rows((1, 3), (tgt, block), (8, rows))


def source_kernel(payload, source, state, relation, ids, ids_next, q_high, q_low, rel_in,
                  new_source, new_state, next_high, next_low, next_rel):
    width = source.shape[0]
    packed = payload[...].astype(jnp.int32)
    high, low = halves(decoded(packed[:width], packed[width : width + 1]))
    stack = jnp.concatenate([high, low, high], axis=1)
    parts = row_major(high, low)
    gradient = jnp.zeros(source.shape, F32)
    for first in range(0, LIVE, CHUNK):
        at = pl.ds(first, CHUNK)
        gh, gl = score_gradients(parts, q_high[:, at], q_low[:, at], ids[1:2, at], ids[3:4, at])
        gradient += source_gradient(stack, gh, gl, rel_in[:, at], ids[0:1, at])
    updated, sums = adagrad(source[...], state[...], gradient)
    new_source[...] = updated
    new_state[...] = sums
    stack = jnp.concatenate(halves(updated), axis=1)
    relation3 = relation_parts(relation[...])
    for first in range(0, LIVE, CHUNK):
        at = pl.ds(first, CHUNK)
        next_high[:, at], next_low[:, at], next_rel[:, at] = queries(
            stack, relation3, ids_next[0:1, at], ids_next[2:3, at])


def slots(shard, changed, top, bottom):
    rows = shard.shape[1]
    is_row = lax.broadcasted_iota(jnp.int32, (8, rows), 0)
    mine = jnp.logical_and(is_row == shard, changed == 1).astype(F32)
    before = lax.broadcasted_iota(jnp.int32, (rows, rows), 0) < lax.broadcasted_iota(jnp.int32, (rows, rows), 1)
    rank = dot(mine.astype(BF16), before.astype(F32).astype(BF16), NN)
    slot = jnp.sum(mine * rank, axis=0, keepdims=True).astype(jnp.int32)
    code = jnp.where(changed == 1, shard * (2 * SLOTS) + slot, -2 * SLOTS)
    top[...] = one_hot(code, top.shape[0])
    bottom[...] = one_hot(code + SLOTS, bottom.shape[0])


def publish(updated, top, bottom, outgoing):
    width, rows = updated.shape
    half = width // 2
    number = (lax.broadcasted_iota(jnp.int32, (8, rows), 1) + 1).astype(F32)
    packed = dot(
        jnp.concatenate([jnp.concatenate([updated[:half], number], axis=0).astype(BF16),
                         jnp.concatenate([updated[half:], number], axis=0).astype(BF16)], axis=1),
        jnp.concatenate([top, bottom], axis=1), NT).astype(BF16)
    for s in range(outgoing.shape[0]):
        outgoing[s] = packed[:, s * 2 * SLOTS : (s + 1) * 2 * SLOTS]


def main_kernel(payload, behind_high, behind_low, behind_ids, source, state, ids, q_high, q_low, rel_in, top, bottom,
                new_source, new_state, new_target, new_target_state, g_high, g_low, outgoing):
    width, rows = source.shape
    packed = payload[...].astype(jnp.int32)
    target = decoded(packed[:width], packed[width : width + 1])
    tail = packed[width:].astype(F32)
    target_state = (tail[1:2] + tail[2:3] * (1.0 / SCALE_UNIT)) * (1.0 / SCALE_UNIT)
    parts = row_major(*halves(target))
    gradient = jnp.zeros(source.shape, F32)
    for first in range(0, LIVE, CHUNK):
        at = pl.ds(first, CHUNK)
        qh, ql = behind_high[:, at], behind_low[:, at]
        gh, gl = score_gradients(parts, qh, ql, behind_ids[1:2, at], behind_ids[3:4, at])
        gradient += target_gradient(qh, ql, gh, gl)
    target, sums = adagrad(target, target_state, gradient)
    new_target[...] = target
    new_target_state[...] = sums
    high, low = halves(target)
    stack = jnp.concatenate([high, low, high], axis=1)
    parts = row_major(high, low)
    gradient = jnp.zeros(source.shape, F32)
    for first in range(0, LIVE, CHUNK):
        at = pl.ds(first, CHUNK)
        gh, gl = score_gradients(parts, q_high[:, at], q_low[:, at], ids[1:2, at], ids[3:4, at])
        g_high[:, at] = gh
        g_low[:, at] = gl
        gradient += source_gradient(stack, gh, gl, rel_in[:, at], ids[0:1, at])
    updated, sums = adagrad(source[...], state[...], gradient)
    new_source[...] = updated
    new_state[...] = sums
    publish(updated, top[...], bottom[...], outgoing)


def last_target_kernel(target, state, q_high, q_low, g_high, g_low, new_target, new_state):
    gradient = jnp.zeros(target.shape, F32)
    for first in range(0, LIVE, CHUNK):
        at = pl.ds(first, CHUNK)
        gradient += target_gradient(q_high[:, at], q_low[:, at], g_high[:, at], g_low[:, at])
    new_target[...], new_state[...] = adagrad(target[...], state[...], gradient)


def serve_kernel(incoming, served):
    shards, packed_rows, lanes = incoming.shape
    half = served.shape[1] // 2
    rows = served.shape[2]
    lane = lax.broadcasted_iota(jnp.int32, (rows, lanes), 1)
    number = (lax.broadcasted_iota(jnp.int32, (rows, lanes), 0) + 1).astype(F32)
    for s in range(shards):
        block = incoming[s]
        index = block[half : half + 8].astype(F32)[:1]
        match = number == index
        top = jnp.logical_and(match, lane < SLOTS).astype(F32)
        bottom = jnp.logical_and(match, lane >= SLOTS).astype(F32)
        spread = dot(block, jnp.concatenate([top, bottom], axis=0).astype(BF16), NT)
        served[s] = jnp.concatenate([spread[:half, :rows], spread[:half, rows:]], axis=0).astype(BF16)


VMEM = pl.BlockSpec(memory_space=pltpu.VMEM)
SMEM = pl.BlockSpec(memory_space=pltpu.SMEM)


def call(kernel, outs, args, scalars=(), flops=10**9):
    return pl.pallas_call(
        kernel,
        out_shape=[jax.ShapeDtypeStruct(shape, kind) for shape, kind in outs],
        in_specs=[SMEM if i in scalars else VMEM for i in range(len(args))],
        out_specs=[VMEM] * len(outs),
        compiler_params=pltpu.CompilerParams(vmem_limit_bytes=40 * 2**20),
        cost_estimate=pl.CostEstimate(flops=flops, bytes_accessed=2**16, transcendentals=0),
    )(*args)


def from_behind(block, axis, distance):
    devices = range(lax.axis_size(axis))
    route = [((i - distance) % len(devices), i) for i in devices]
    return lax.ppermute(block, axis, route)


def on_device(
    source_rows,
    source_state,
    target_rows,
    target_state,
    relation_table,
    source_ids,
    target_ids,
    relation_ids,
    negative_block,
    edge_counts,
    serving_shard,
    changed_rows,
):
    source = jnp.swapaxes(source_rows[0, 0], 0, 1)
    target = jnp.swapaxes(target_rows[0, 0], 0, 1)
    source_sums, target_sums = source_state[0], target_state[0]
    src, tgt, rel = source_ids[0, 0], target_ids[0, 0], relation_ids[0, 0]
    negatives, counts = negative_block[0, 0], edge_counts[0, 0]
    width, rows = source.shape
    shards = lax.axis_size("serve")
    matrix, line = ((width, rows), F32), ((1, rows), F32)
    edge16, edge32, grad16 = ((width, LIVE), BF16), ((width, LIVE), F32), ((rows, LIVE), BF16)
    shard, changed = serving_shard[0], changed_rows[0]
    payload, ids8 = ((width + TAIL, rows), jnp.int16), ((8, LIVE), jnp.int32)
    places = ((shards * 2 * SLOTS, rows), BF16)

    near_out = call(encode_target_kernel, [payload], (target,))[0]
    source_out, far_out, ids = call(
        encode_source_kernel, [payload, payload, ids8],
        (source, src, tgt, rel, negatives, counts, near_out, target_sums), (4, 5))
    near_target = from_behind(near_out, "dom", 1)
    near_source = from_behind(source_out, "dom", 1)
    far_target = from_behind(far_out, "dom", 2)
    q_high, q_low, relation, ids_next, top, bottom = call(
        query_kernel, [edge16, edge16, edge32, ids8, places, places],
        (source, relation_table, ids, src, tgt, rel, negatives, counts, shard, changed), (6, 7))
    source, source_sums, q_high, q_low, relation = call(
        source_kernel, [matrix, line, edge16, edge16, edge32],
        (near_target, source, source_sums, relation_table, ids, ids_next, q_high, q_low, relation), flops=8 * 10**9)
    behind_high, behind_low, behind_ids = call(
        behind_kernel, [edge16, edge16, ids8], (near_source, relation_table), flops=10**6)
    source, source_sums, target, target_sums, g_high, g_low, outgoing = call(
        main_kernel, [matrix, line, matrix, line, grad16, grad16, ((shards, width // 2 + 8, 2 * SLOTS), BF16)],
        (far_target, behind_high, behind_low, behind_ids, source, source_sums, ids_next, q_high, q_low, relation, top, bottom))
    incoming = lax.all_to_all(outgoing, "serve", split_axis=0, concat_axis=0, tiled=True)
    target, target_sums = call(last_target_kernel, [matrix, line], (target, target_sums, q_high, q_low, g_high, g_low))
    served = call(serve_kernel, [((shards, width, rows), BF16)], (incoming,))[0]
    return (
        jnp.swapaxes(source, 0, 1)[None, None],
        source_sums[None],
        jnp.swapaxes(target, 0, 1)[None, None],
        target_sums[None],
        jnp.swapaxes(served, 1, 2)[None, None],
    )


def solution(mesh):
    return jax.shard_map(
        on_device,
        mesh=mesh,
        in_specs=(
            P("dom", "serve", None, None),
            P("dom", "serve", None),
            P("dom", "serve", None, None),
            P("dom", "serve", None),
            P(),
            P("dom", "serve", None, None, None),
            P("dom", "serve", None, None, None),
            P("dom", "serve", None, None, None),
            P("dom", "serve", None, None),
            P("dom", "serve", None, None),
            P("dom", "serve", None),
            P("dom", "serve", None),
        ),
        out_specs=(
            P("dom", "serve", None, None),
            P("dom", "serve", None),
            P("dom", "serve", None, None),
            P("dom", "serve", None),
            P("dom", "serve", None, None, None),
        ),
        check_vma=False,
    )
```

```python
import jax
import jax.numpy as jnp
from jax import lax
from jax.experimental import pallas as pl
from jax.experimental.pallas import tpu as pltpu
from jax.sharding import PartitionSpec as P

LEARN_RATE = 0.1
EPSILON = 1e-08
SLOTS = 64

F32 = jnp.float32
BF16 = jnp.bfloat16
NN = ((1,), (0,))
NT = ((1,), (1,))
TN = ((0,), (0,))
LANES = 128
CHUNK = 768
LIVE = 768
SCALE_UNIT = 16384.0
CODE_MAX = 32767.0
TAIL = 16


def dot(a, b, dims):
    return lax.dot_general(a, b, (dims, ((), ())), preferred_element_type=F32)


def halves(x):
    high = x.astype(BF16)
    return high, (x - high.astype(F32)).astype(BF16)


def sigmoid(x):
    return 0.5 + 0.5 * jnp.tanh(0.5 * x)


def one_hot(ids, rows):
    place = lax.broadcasted_iota(jnp.int32, (rows, ids.shape[1]), 0)
    return (place == ids).astype(F32).astype(BF16)


def compact(step, src_ref, tgt_ref, rel_ref, nb_ref, count_ref):
    blocks, lanes = src_ref.shape[1:]
    stack = jnp.concatenate([src_ref[step], tgt_ref[step], rel_ref[step], jnp.zeros_like(src_ref[step])], axis=0)
    stack = stack.astype(F32)
    row = lax.broadcasted_iota(jnp.int32, stack.shape, 0)
    edge = lax.broadcasted_iota(jnp.int32, (lanes, LIVE), 0)
    apart = lax.broadcasted_iota(jnp.int32, (lanes, LIVE), 1) - edge
    packed = jnp.zeros((stack.shape[0], LIVE), F32)
    start = 0
    for b in range(blocks):
        count = count_ref[step, b]
        block = nb_ref[step, b].astype(F32)
        mine = jnp.where(row % blocks == b, stack + jnp.where(row >= 3 * blocks, block, 0.0), 0.0)
        to = jnp.logical_and(apart == start, edge < count)
        packed += dot(mine.astype(BF16), to.astype(F32).astype(BF16), NN)
        start = start + count
    return [
        jnp.sum(packed[i * blocks : (i + 1) * blocks], axis=0, keepdims=True).astype(jnp.int32) for i in range(4)
    ]


def pick_rows(rows, values, shape):
    row = lax.broadcasted_iota(jnp.int32, shape, 0)
    out = jnp.zeros(shape, jnp.int32)
    for i, value in zip(rows, values):
        out = jnp.where(row == i, value, out)
    return out


def coded(x):
    largest = jnp.max(jnp.abs(x), axis=0, keepdims=True)
    unit = jnp.floor(largest * SCALE_UNIT) + 1.0
    code = jnp.floor(x * ((CODE_MAX * SCALE_UNIT) / unit) + 0.5)
    return code.astype(jnp.int32), unit.astype(jnp.int32)


def decoded(codes, unit):
    return codes.astype(F32) * (unit.astype(F32) * (1.0 / (CODE_MAX * SCALE_UNIT)))


def relation_parts(relation):
    high = relation.astype(BF16)
    rest = relation - high.astype(F32)
    middle = rest.astype(BF16)
    low = (rest - middle.astype(F32)).astype(BF16)
    return jnp.concatenate([high, middle, low], axis=0)


def queries(source_stack, relation3, src, rel):
    relations = relation3.shape[0] // 3
    rows = one_hot(src, source_stack.shape[1] // 2)
    pick = one_hot(rel, relations)
    relation = dot(relation3, jnp.concatenate([pick, pick, pick], axis=0), TN)
    qh, ql = halves(dot(source_stack, jnp.concatenate([rows, rows], axis=0), NN) * relation)
    return qh, ql, relation


def score_gradients(target_parts, qh, ql, tgt, block):
    rows = target_parts.shape[0]
    lanes = tgt.shape[1]
    scores = dot(target_parts, jnp.concatenate([qh, qh, ql], axis=0), NN)
    hit = lax.broadcasted_iota(jnp.int32, (rows, lanes), 0) == tgt
    positive = jnp.sum(jnp.where(hit, scores, 0.0), axis=0, keepdims=True)
    dpos = -sigmoid(-positive)
    upper = jnp.broadcast_to(block, (LANES, lanes)) == 0
    negative = jnp.where(upper, scores[:LANES], scores[LANES:])
    dneg = sigmoid(negative) * (1.0 / LANES)
    spread = jnp.concatenate([jnp.where(upper, dneg, 0.0), jnp.where(upper, 0.0, dneg)], axis=0)
    return halves(spread + jnp.where(hit, dpos, 0.0))


def row_major(high, low):
    return jnp.concatenate([high.T, low.T, high.T], axis=1)


def adagrad(weights, state, gradient):
    new_state = state + jnp.sum(gradient * gradient, axis=0, keepdims=True) * (1.0 / gradient.shape[0])
    scale = LEARN_RATE / (jnp.sqrt(new_state) + EPSILON)
    return weights - gradient * scale, new_state


def target_gradient(qh, ql, gh, gl):
    return dot(jnp.concatenate([qh, ql, qh], axis=1), jnp.concatenate([gh, gh, gl], axis=1), NT)


def source_gradient(target_stack, gh, gl, relation, src):
    flow = dot(target_stack, jnp.concatenate([gh, gh, gl], axis=0), NN) * relation
    rows = one_hot(src, gh.shape[0])
    return dot(jnp.concatenate(halves(flow), axis=1), jnp.concatenate([rows, rows], axis=1), NT)


def encode_target_kernel(target, payload):
    codes, unit = coded(target[...])
    tail = pick_rows((0,), [unit], (TAIL, target.shape[1]))
    payload[...] = jnp.concatenate([codes, tail], axis=0).astype(jnp.int16)


def encode_source_kernel(source, src, tgt, rel, nb_ref, count_ref, near, state, payload, far, ids_now):
    width, rows = source.shape
    codes, unit = coded(source[...])
    ids = compact(0, src, tgt, rel, nb_ref, count_ref)
    ids_now[...] = pick_rows(range(4), ids, ids_now.shape)
    pieces = [i[:, at : at + rows] for i in ids for at in range(0, LIVE, rows)]
    tail = pick_rows(range(TAIL), [unit] + pieces, (TAIL, rows))
    payload[...] = jnp.concatenate([codes, tail], axis=0).astype(jnp.int16)
    scaled = state[...] * SCALE_UNIT
    whole = jnp.floor(scaled)
    part = jnp.floor((scaled - whole) * SCALE_UNIT + 0.5)
    unit = near[width : width + TAIL].astype(jnp.int32)[:1]
    tail = pick_rows(range(3), [unit, whole.astype(jnp.int32), part.astype(jnp.int32)], (TAIL, rows))
    far[:width] = near[:width]
    far[width:] = tail.astype(jnp.int16)


def query_kernel(source, relation, ids, src_ref, tgt_ref, rel_ref, nb_ref, count_ref, shard, changed,
                 q_high, q_low, rel_out, ids_next, top, bottom):
    stack = jnp.concatenate(halves(source[...]), axis=1)
    relation3 = relation_parts(relation[...])
    for first in range(0, LIVE, CHUNK):
        at = pl.ds(first, CHUNK)
        q_high[:, at], q_low[:, at], rel_out[:, at] = queries(stack, relation3, ids[0:1, at], ids[2:3, at])
    ids_next[...] = pick_rows(range(4), compact(1, src_ref, tgt_ref, rel_ref, nb_ref, count_ref), ids_next.shape)
    slots(shard[...], changed[...], top, bottom)


def behind_kernel(payload, relation, q_high, q_low, ids):
    width, rows = payload.shape[0] - TAIL, payload.shape[1]
    packed = payload[...].astype(jnp.int32)
    tail = packed[width:]
    stack = jnp.concatenate(halves(decoded(packed[:width], tail[0:1])), axis=1)
    relation3 = relation_parts(relation[...])
    pieces = LIVE // rows
    for i in range(pieces):
        at = pl.ds(i * rows, rows)
        src, tgt, rel, block = [tail[1 + j * pieces + i : 2 + j * pieces + i] for j in range(4)]
        q_high[:, at], q_low[:, at], _ = queries(stack, relation3, src, rel)
        ids[:, at] = pick_rows((1, 3), (tgt, block), (8, rows))


def source_kernel(payload, source, state, relation, ids, ids_next, q_high, q_low, rel_in,
                  new_source, new_state, next_high, next_low, next_rel):
    width = source.shape[0]
    packed = payload[...].astype(jnp.int32)
    high, low = halves(decoded(packed[:width], packed[width : width + 1]))
    stack = jnp.concatenate([high, low, high], axis=1)
    parts = row_major(high, low)
    gradient = jnp.zeros(source.shape, F32)
    for first in range(0, LIVE, CHUNK):
        at = pl.ds(first, CHUNK)
        gh, gl = score_gradients(parts, q_high[:, at], q_low[:, at], ids[1:2, at], ids[3:4, at])
        gradient += source_gradient(stack, gh, gl, rel_in[:, at], ids[0:1, at])
    updated, sums = adagrad(source[...], state[...], gradient)
    new_source[...] = updated
    new_state[...] = sums
    stack = jnp.concatenate(halves(updated), axis=1)
    relation3 = relation_parts(relation[...])
    for first in range(0, LIVE, CHUNK):
        at = pl.ds(first, CHUNK)
        next_high[:, at], next_low[:, at], next_rel[:, at] = queries(
            stack, relation3, ids_next[0:1, at], ids_next[2:3, at])


def slots(shard, changed, top, bottom):
    rows = shard.shape[1]
    is_row = lax.broadcasted_iota(jnp.int32, (8, rows), 0)
    mine = jnp.logical_and(is_row == shard, changed == 1).astype(F32)
    before = lax.broadcasted_iota(jnp.int32, (rows, rows), 0) < lax.broadcasted_iota(jnp.int32, (rows, rows), 1)
    rank = dot(mine.astype(BF16), before.astype(F32).astype(BF16), NN)
    slot = jnp.sum(mine * rank, axis=0, keepdims=True).astype(jnp.int32)
    code = jnp.where(changed == 1, shard * (2 * SLOTS) + slot, -2 * SLOTS)
    top[...] = one_hot(code, top.shape[0])
    bottom[...] = one_hot(code + SLOTS, bottom.shape[0])


def publish(updated, top, bottom, outgoing):
    width, rows = updated.shape
    half = width // 2
    number = (lax.broadcasted_iota(jnp.int32, (8, rows), 1) + 1).astype(F32)
    packed = dot(
        jnp.concatenate([jnp.concatenate([updated[:half], number], axis=0).astype(BF16),
                         jnp.concatenate([updated[half:], number], axis=0).astype(BF16)], axis=1),
        jnp.concatenate([top, bottom], axis=1), NT).astype(BF16)
    for s in range(outgoing.shape[0]):
        outgoing[s] = packed[:, s * 2 * SLOTS : (s + 1) * 2 * SLOTS]


def main_kernel(payload, behind_high, behind_low, behind_ids, source, state, ids, q_high, q_low, rel_in, top, bottom,
                new_source, new_state, new_target, new_target_state, g_high, g_low, outgoing):
    width, rows = source.shape
    packed = payload[...].astype(jnp.int32)
    target = decoded(packed[:width], packed[width : width + 1])
    tail = packed[width:].astype(F32)
    target_state = (tail[1:2] + tail[2:3] * (1.0 / SCALE_UNIT)) * (1.0 / SCALE_UNIT)
    parts = row_major(*halves(target))
    gradient = jnp.zeros(source.shape, F32)
    for first in range(0, LIVE, CHUNK):
        at = pl.ds(first, CHUNK)
        qh, ql = behind_high[:, at], behind_low[:, at]
        gh, gl = score_gradients(parts, qh, ql, behind_ids[1:2, at], behind_ids[3:4, at])
        gradient += target_gradient(qh, ql, gh, gl)
    target, sums = adagrad(target, target_state, gradient)
    new_target[...] = target
    new_target_state[...] = sums
    high, low = halves(target)
    stack = jnp.concatenate([high, low, high], axis=1)
    parts = row_major(high, low)
    gradient = jnp.zeros(source.shape, F32)
    for first in range(0, LIVE, CHUNK):
        at = pl.ds(first, CHUNK)
        gh, gl = score_gradients(parts, q_high[:, at], q_low[:, at], ids[1:2, at], ids[3:4, at])
        g_high[:, at] = gh
        g_low[:, at] = gl
        gradient += source_gradient(stack, gh, gl, rel_in[:, at], ids[0:1, at])
    updated, sums = adagrad(source[...], state[...], gradient)
    new_source[...] = updated
    new_state[...] = sums
    publish(updated, top[...], bottom[...], outgoing)


def last_target_kernel(target, state, q_high, q_low, g_high, g_low, source, source_state,
                       new_target, new_state, new_source, new_source_state):
    new_source[...] = source[...]
    new_source_state[...] = source_state[...]
    gradient = jnp.zeros(target.shape, F32)
    for first in range(0, LIVE, CHUNK):
        at = pl.ds(first, CHUNK)
        gradient += target_gradient(q_high[:, at], q_low[:, at], g_high[:, at], g_low[:, at])
    new_target[...], new_state[...] = adagrad(target[...], state[...], gradient)


def serve_kernel(incoming, served, spread, sems):
    shards, packed_rows, lanes = incoming.shape
    half = spread.shape[1] // 2
    rows = spread.shape[2]
    lane = lax.broadcasted_iota(jnp.int32, (rows, lanes), 1)
    number = (lax.broadcasted_iota(jnp.int32, (rows, lanes), 0) + 1).astype(F32)
    copies = []
    for s in range(shards):
        block = incoming[s]
        match = number == block[half : half + 8].astype(F32)[:1]
        top = jnp.logical_and(match, lane < SLOTS).astype(F32)
        bottom = jnp.logical_and(match, lane >= SLOTS).astype(F32)
        both = dot(block, jnp.concatenate([top, bottom], axis=0).astype(BF16), NT)
        spread[s] = jnp.concatenate([both[:half, :rows], both[:half, rows:]], axis=0).astype(BF16)
        copies.append(pltpu.make_async_copy(spread.at[s], served.at[s], sems.at[s]))
        copies[-1].start()
    for copy in copies:
        copy.wait()


VMEM = pl.BlockSpec(memory_space=pltpu.VMEM)
SMEM = pl.BlockSpec(memory_space=pltpu.SMEM)


def call(kernel, outs, args, scalars=(), flops=10**9):
    return pl.pallas_call(
        kernel,
        out_shape=[jax.ShapeDtypeStruct(shape, kind) for shape, kind in outs],
        in_specs=[SMEM if i in scalars else VMEM for i in range(len(args))],
        out_specs=[VMEM] * len(outs),
        compiler_params=pltpu.CompilerParams(vmem_limit_bytes=40 * 2**20),
        cost_estimate=pl.CostEstimate(flops=flops, bytes_accessed=2**16, transcendentals=0),
    )(*args)


def from_behind(block, axis, distance):
    devices = range(lax.axis_size(axis))
    route = [((i - distance) % len(devices), i) for i in devices]
    return lax.ppermute(block, axis, route)


def on_device(
    source_rows,
    source_state,
    target_rows,
    target_state,
    relation_table,
    source_ids,
    target_ids,
    relation_ids,
    negative_block,
    edge_counts,
    serving_shard,
    changed_rows,
):
    source = jnp.swapaxes(source_rows[0, 0], 0, 1)
    target = jnp.swapaxes(target_rows[0, 0], 0, 1)
    source_sums, target_sums = source_state[0], target_state[0]
    src, tgt, rel = source_ids[0, 0], target_ids[0, 0], relation_ids[0, 0]
    negatives, counts = negative_block[0, 0], edge_counts[0, 0]
    width, rows = source.shape
    shards = lax.axis_size("serve")
    matrix, line = ((width, rows), F32), ((1, rows), F32)
    edge16, edge32, grad16 = ((width, LIVE), BF16), ((width, LIVE), F32), ((rows, LIVE), BF16)
    shard, changed = serving_shard[0], changed_rows[0]
    payload, ids8 = ((width + TAIL, rows), jnp.int16), ((8, LIVE), jnp.int32)
    places = ((shards * 2 * SLOTS, rows), BF16)

    near_out = call(encode_target_kernel, [payload], (target,))[0]
    source_out, far_out, ids = call(
        encode_source_kernel, [payload, payload, ids8],
        (source, src, tgt, rel, negatives, counts, near_out, target_sums), (4, 5))
    near_target = from_behind(near_out, "dom", 1)
    near_source = from_behind(source_out, "dom", 1)
    far_target = from_behind(far_out, "dom", 2)
    q_high, q_low, relation, ids_next, top, bottom = call(
        query_kernel, [edge16, edge16, edge32, ids8, places, places],
        (source, relation_table, ids, src, tgt, rel, negatives, counts, shard, changed), (6, 7))
    source, source_sums, q_high, q_low, relation = call(
        source_kernel, [matrix, line, edge16, edge16, edge32],
        (near_target, source, source_sums, relation_table, ids, ids_next, q_high, q_low, relation), flops=8 * 10**9)
    behind_high, behind_low, behind_ids = call(
        behind_kernel, [edge16, edge16, ids8], (near_source, relation_table), flops=10**6)
    source, source_sums, target, target_sums, g_high, g_low, outgoing = call(
        main_kernel, [matrix, line, matrix, line, grad16, grad16, ((shards, width // 2 + 8, 2 * SLOTS), BF16)],
        (far_target, behind_high, behind_low, behind_ids, source, source_sums, ids_next, q_high, q_low, relation, top, bottom))
    incoming = lax.all_to_all(outgoing, "serve", split_axis=0, concat_axis=0, tiled=True)
    target, target_sums, source, source_sums = call(
        last_target_kernel, [matrix, line, matrix, line],
        (target, target_sums, q_high, q_low, g_high, g_low, source, source_sums))
    served = pl.pallas_call(
        serve_kernel,
        out_shape=jax.ShapeDtypeStruct((shards, width, rows), BF16),
        in_specs=[VMEM],
        out_specs=pl.BlockSpec(memory_space=pl.ANY),
        scratch_shapes=[pltpu.VMEM((shards, width, rows), BF16), pltpu.SemaphoreType.DMA((shards,))],
        compiler_params=pltpu.CompilerParams(vmem_limit_bytes=40 * 2**20),
    )(incoming)
    return (
        jnp.swapaxes(source, 0, 1)[None, None],
        source_sums[None],
        jnp.swapaxes(target, 0, 1)[None, None],
        target_sums[None],
        jnp.swapaxes(served, 1, 2)[None, None],
    )


def solution(mesh):
    return jax.shard_map(
        on_device,
        mesh=mesh,
        in_specs=(
            P("dom", "serve", None, None),
            P("dom", "serve", None),
            P("dom", "serve", None, None),
            P("dom", "serve", None),
            P(),
            P("dom", "serve", None, None, None),
            P("dom", "serve", None, None, None),
            P("dom", "serve", None, None, None),
            P("dom", "serve", None, None),
            P("dom", "serve", None, None),
            P("dom", "serve", None),
            P("dom", "serve", None),
        ),
        out_specs=(
            P("dom", "serve", None, None),
            P("dom", "serve", None),
            P("dom", "serve", None, None),
            P("dom", "serve", None),
            P("dom", "serve", None, None, None),
        ),
        check_vma=False,
    )
```

```python
import jax
import jax.numpy as jnp
from jax import lax
from jax.experimental import pallas as pl
from jax.experimental.pallas import tpu as pltpu
from jax.sharding import PartitionSpec as P

LEARN_RATE = 0.1
EPSILON = 1e-08
SLOTS = 64

F32 = jnp.float32
BF16 = jnp.bfloat16
NN = ((1,), (0,))
NT = ((1,), (1,))
TN = ((0,), (0,))
LANES = 128
CHUNK = 768
LIVE = 768
SCALE_UNIT = 16384.0
CODE_MAX = 32767.0
TAIL = 16


def dot(a, b, dims):
    return lax.dot_general(a, b, (dims, ((), ())), preferred_element_type=F32)


def halves(x):
    high = x.astype(BF16)
    return high, (x - high.astype(F32)).astype(BF16)


def sigmoid(x):
    return 0.5 + 0.5 * jnp.tanh(0.5 * x)


def one_hot(ids, rows):
    place = lax.broadcasted_iota(jnp.int32, (rows, ids.shape[1]), 0)
    return (place == ids).astype(F32).astype(BF16)


def compact(step, src_ref, tgt_ref, rel_ref, nb_ref, count_ref):
    blocks, lanes = src_ref.shape[1:]
    stack = jnp.concatenate([src_ref[step], tgt_ref[step], rel_ref[step], jnp.zeros_like(src_ref[step])], axis=0)
    stack = stack.astype(F32)
    row = lax.broadcasted_iota(jnp.int32, stack.shape, 0)
    edge = lax.broadcasted_iota(jnp.int32, (lanes, LIVE), 0)
    apart = lax.broadcasted_iota(jnp.int32, (lanes, LIVE), 1) - edge
    packed = jnp.zeros((stack.shape[0], LIVE), F32)
    start = 0
    for b in range(blocks):
        count = count_ref[step, b]
        block = nb_ref[step, b].astype(F32)
        mine = jnp.where(row % blocks == b, stack + jnp.where(row >= 3 * blocks, block, 0.0), 0.0)
        to = jnp.logical_and(apart == start, edge < count)
        packed += dot(mine.astype(BF16), to.astype(F32).astype(BF16), NN)
        start = start + count
    return [
        jnp.sum(packed[i * blocks : (i + 1) * blocks], axis=0, keepdims=True).astype(jnp.int32) for i in range(4)
    ]


def pick_rows(rows, values, shape):
    row = lax.broadcasted_iota(jnp.int32, shape, 0)
    out = jnp.zeros(shape, jnp.int32)
    for i, value in zip(rows, values):
        out = jnp.where(row == i, value, out)
    return out


def coded(x):
    largest = jnp.max(jnp.abs(x), axis=0, keepdims=True)
    unit = jnp.floor(largest * SCALE_UNIT) + 1.0
    code = jnp.floor(x * ((CODE_MAX * SCALE_UNIT) / unit) + 0.5)
    return code.astype(jnp.int32), unit.astype(jnp.int32)


def decoded(codes, unit):
    return codes.astype(F32) * (unit.astype(F32) * (1.0 / (CODE_MAX * SCALE_UNIT)))


def relation_parts(relation):
    high = relation.astype(BF16)
    rest = relation - high.astype(F32)
    middle = rest.astype(BF16)
    low = (rest - middle.astype(F32)).astype(BF16)
    return jnp.concatenate([high, middle, low], axis=0)


def queries(source_stack, relation3, src, rel):
    relations = relation3.shape[0] // 3
    rows = one_hot(src, source_stack.shape[1] // 2)
    pick = one_hot(rel, relations)
    relation = dot(relation3, jnp.concatenate([pick, pick, pick], axis=0), TN)
    qh, ql = halves(dot(source_stack, jnp.concatenate([rows, rows], axis=0), NN) * relation)
    return qh, ql, relation


def score_gradients(target_parts, qh, ql, tgt, block):
    rows = target_parts.shape[0]
    lanes = tgt.shape[1]
    scores = dot(target_parts, jnp.concatenate([qh, qh, ql], axis=0), NN)
    hit = lax.broadcasted_iota(jnp.int32, (rows, lanes), 0) == tgt
    positive = jnp.sum(jnp.where(hit, scores, 0.0), axis=0, keepdims=True)
    dpos = -sigmoid(-positive)
    upper = jnp.broadcast_to(block, (LANES, lanes)) == 0
    negative = jnp.where(upper, scores[:LANES], scores[LANES:])
    dneg = sigmoid(negative) * (1.0 / LANES)
    spread = jnp.concatenate([jnp.where(upper, dneg, 0.0), jnp.where(upper, 0.0, dneg)], axis=0)
    return halves(spread + jnp.where(hit, dpos, 0.0))


def row_major(high, low):
    return jnp.concatenate([high.T, low.T, high.T], axis=1)


def adagrad(weights, state, gradient):
    new_state = state + jnp.sum(gradient * gradient, axis=0, keepdims=True) * (1.0 / gradient.shape[0])
    scale = LEARN_RATE / (jnp.sqrt(new_state) + EPSILON)
    return weights - gradient * scale, new_state


def target_gradient(qh, ql, gh, gl):
    return dot(jnp.concatenate([qh, ql, qh], axis=1), jnp.concatenate([gh, gh, gl], axis=1), NT)


def source_gradient(target_stack, gh, gl, relation, src):
    flow = dot(target_stack, jnp.concatenate([gh, gh, gl], axis=0), NN) * relation
    rows = one_hot(src, gh.shape[0])
    return dot(jnp.concatenate(halves(flow), axis=1), jnp.concatenate([rows, rows], axis=1), NT)


def encode_target_kernel(target, payload):
    codes, unit = coded(target[...])
    tail = pick_rows((0,), [unit], (TAIL, target.shape[1]))
    payload[...] = jnp.concatenate([codes, tail], axis=0).astype(jnp.int16)


def encode_source_kernel(source, src, tgt, rel, nb_ref, count_ref, near, state, payload, far, ids_now):
    width, rows = source.shape
    codes, unit = coded(source[...])
    ids = compact(0, src, tgt, rel, nb_ref, count_ref)
    ids_now[...] = pick_rows(range(4), ids, ids_now.shape)
    pieces = [i[:, at : at + rows] for i in ids for at in range(0, LIVE, rows)]
    tail = pick_rows(range(TAIL), [unit] + pieces, (TAIL, rows))
    payload[...] = jnp.concatenate([codes, tail], axis=0).astype(jnp.int16)
    scaled = state[...] * SCALE_UNIT
    whole = jnp.floor(scaled)
    part = jnp.floor((scaled - whole) * SCALE_UNIT + 0.5)
    unit = near[width : width + TAIL].astype(jnp.int32)[:1]
    tail = pick_rows(range(3), [unit, whole.astype(jnp.int32), part.astype(jnp.int32)], (TAIL, rows))
    far[:width] = near[:width]
    far[width:] = tail.astype(jnp.int16)


def query_kernel(source, relation, ids, src_ref, tgt_ref, rel_ref, nb_ref, count_ref, shard, changed,
                 q_high, q_low, rel_out, ids_next, top, bottom):
    stack = jnp.concatenate(halves(source[...]), axis=1)
    relation3 = relation_parts(relation[...])
    for first in range(0, LIVE, CHUNK):
        at = pl.ds(first, CHUNK)
        q_high[:, at], q_low[:, at], rel_out[:, at] = queries(stack, relation3, ids[0:1, at], ids[2:3, at])
    ids_next[...] = pick_rows(range(4), compact(1, src_ref, tgt_ref, rel_ref, nb_ref, count_ref), ids_next.shape)
    slots(shard[...], changed[...], top, bottom)


def behind_kernel(payload, relation, q_high, q_low, ids):
    width, rows = payload.shape[0] - TAIL, payload.shape[1]
    packed = payload[...].astype(jnp.int32)
    tail = packed[width:]
    stack = jnp.concatenate(halves(decoded(packed[:width], tail[0:1])), axis=1)
    relation3 = relation_parts(relation[...])
    pieces = LIVE // rows
    for i in range(pieces):
        at = pl.ds(i * rows, rows)
        src, tgt, rel, block = [tail[1 + j * pieces + i : 2 + j * pieces + i] for j in range(4)]
        q_high[:, at], q_low[:, at], _ = queries(stack, relation3, src, rel)
        ids[:, at] = pick_rows((1, 3), (tgt, block), (8, rows))


def source_kernel(payload, source, state, relation, ids, ids_next, q_high, q_low, rel_in,
                  new_source, new_state, next_high, next_low, next_rel):
    width = source.shape[0]
    packed = payload[...].astype(jnp.int32)
    high, low = halves(decoded(packed[:width], packed[width : width + 1]))
    stack = jnp.concatenate([high, low, high], axis=1)
    parts = row_major(high, low)
    gradient = jnp.zeros(source.shape, F32)
    for first in range(0, LIVE, CHUNK):
        at = pl.ds(first, CHUNK)
        gh, gl = score_gradients(parts, q_high[:, at], q_low[:, at], ids[1:2, at], ids[3:4, at])
        gradient += source_gradient(stack, gh, gl, rel_in[:, at], ids[0:1, at])
    updated, sums = adagrad(source[...], state[...], gradient)
    new_source[...] = updated
    new_state[...] = sums
    stack = jnp.concatenate(halves(updated), axis=1)
    relation3 = relation_parts(relation[...])
    for first in range(0, LIVE, CHUNK):
        at = pl.ds(first, CHUNK)
        next_high[:, at], next_low[:, at], next_rel[:, at] = queries(
            stack, relation3, ids_next[0:1, at], ids_next[2:3, at])


def slots(shard, changed, top, bottom):
    rows = shard.shape[1]
    is_row = lax.broadcasted_iota(jnp.int32, (8, rows), 0)
    mine = jnp.logical_and(is_row == shard, changed == 1).astype(F32)
    before = lax.broadcasted_iota(jnp.int32, (rows, rows), 0) < lax.broadcasted_iota(jnp.int32, (rows, rows), 1)
    rank = dot(mine.astype(BF16), before.astype(F32).astype(BF16), NN)
    slot = jnp.sum(mine * rank, axis=0, keepdims=True).astype(jnp.int32)
    code = jnp.where(changed == 1, shard * (2 * SLOTS) + slot, -2 * SLOTS)
    top[...] = one_hot(code, top.shape[0])
    bottom[...] = one_hot(code + SLOTS, bottom.shape[0])


def publish(updated, top, bottom, outgoing):
    width, rows = updated.shape
    half = width // 2
    number = (lax.broadcasted_iota(jnp.int32, (8, rows), 1) + 1).astype(F32)
    packed = dot(
        jnp.concatenate([jnp.concatenate([updated[:half], number], axis=0).astype(BF16),
                         jnp.concatenate([updated[half:], number], axis=0).astype(BF16)], axis=1),
        jnp.concatenate([top, bottom], axis=1), NT).astype(BF16)
    for s in range(outgoing.shape[0]):
        outgoing[s] = packed[:, s * 2 * SLOTS : (s + 1) * 2 * SLOTS]


def far_kernel(payload, target, state, parts):
    width = target.shape[0]
    packed = payload[...].astype(jnp.int32)
    rows = decoded(packed[:width], packed[width : width + 1])
    tail = packed[width:].astype(F32)
    state[...] = (tail[1:2] + tail[2:3] * (1.0 / SCALE_UNIT)) * (1.0 / SCALE_UNIT)
    target[...] = rows
    parts[...] = row_major(*halves(rows))


def main_kernel(far_target, far_state, far_parts, behind_high, behind_low, behind_ids, source, state, ids, q_high, q_low, rel_in, top, bottom,
                new_source, new_state, new_target, new_target_state, g_high, g_low, outgoing):
    parts = far_parts[...]
    gradient = jnp.zeros(source.shape, F32)
    for first in range(0, LIVE, CHUNK):
        at = pl.ds(first, CHUNK)
        qh, ql = behind_high[:, at], behind_low[:, at]
        gh, gl = score_gradients(parts, qh, ql, behind_ids[1:2, at], behind_ids[3:4, at])
        gradient += target_gradient(qh, ql, gh, gl)
    target, sums = adagrad(far_target[...], far_state[...], gradient)
    new_target[...] = target
    new_target_state[...] = sums
    high, low = halves(target)
    stack = jnp.concatenate([high, low, high], axis=1)
    parts = row_major(high, low)
    gradient = jnp.zeros(source.shape, F32)
    for first in range(0, LIVE, CHUNK):
        at = pl.ds(first, CHUNK)
        gh, gl = score_gradients(parts, q_high[:, at], q_low[:, at], ids[1:2, at], ids[3:4, at])
        g_high[:, at] = gh
        g_low[:, at] = gl
        gradient += source_gradient(stack, gh, gl, rel_in[:, at], ids[0:1, at])
    updated, sums = adagrad(source[...], state[...], gradient)
    new_source[...] = updated
    new_state[...] = sums
    publish(updated, top[...], bottom[...], outgoing)


def last_target_kernel(target, state, q_high, q_low, g_high, g_low, source, source_state,
                       new_target, new_state, new_source, new_source_state):
    new_source[...] = source[...]
    new_source_state[...] = source_state[...]
    gradient = jnp.zeros(target.shape, F32)
    for first in range(0, LIVE, CHUNK):
        at = pl.ds(first, CHUNK)
        gradient += target_gradient(q_high[:, at], q_low[:, at], g_high[:, at], g_low[:, at])
    new_target[...], new_state[...] = adagrad(target[...], state[...], gradient)


def serve_kernel(incoming, served, spread, sems):
    shards, packed_rows, lanes = incoming.shape
    half = spread.shape[1] // 2
    rows = spread.shape[2]
    lane = lax.broadcasted_iota(jnp.int32, (rows, lanes), 1)
    number = (lax.broadcasted_iota(jnp.int32, (rows, lanes), 0) + 1).astype(F32)
    copies = []
    for s in range(shards):
        block = incoming[s]
        match = number == block[half : half + 8].astype(F32)[:1]
        top = jnp.logical_and(match, lane < SLOTS).astype(F32)
        bottom = jnp.logical_and(match, lane >= SLOTS).astype(F32)
        both = dot(block, jnp.concatenate([top, bottom], axis=0).astype(BF16), NT)
        spread[s] = jnp.concatenate([both[:half, :rows], both[:half, rows:]], axis=0).astype(BF16)
        copies.append(pltpu.make_async_copy(spread.at[s], served.at[s], sems.at[s]))
        copies[-1].start()
    for copy in copies:
        copy.wait()


VMEM = pl.BlockSpec(memory_space=pltpu.VMEM)
SMEM = pl.BlockSpec(memory_space=pltpu.SMEM)


def call(kernel, outs, args, scalars=(), flops=10**9):
    return pl.pallas_call(
        kernel,
        out_shape=[jax.ShapeDtypeStruct(shape, kind) for shape, kind in outs],
        in_specs=[SMEM if i in scalars else VMEM for i in range(len(args))],
        out_specs=[VMEM] * len(outs),
        compiler_params=pltpu.CompilerParams(vmem_limit_bytes=40 * 2**20),
        cost_estimate=pl.CostEstimate(flops=flops, bytes_accessed=2**16, transcendentals=0),
    )(*args)


def from_behind(block, axis, distance):
    devices = range(lax.axis_size(axis))
    route = [((i - distance) % len(devices), i) for i in devices]
    return lax.ppermute(block, axis, route)


def on_device(
    source_rows,
    source_state,
    target_rows,
    target_state,
    relation_table,
    source_ids,
    target_ids,
    relation_ids,
    negative_block,
    edge_counts,
    serving_shard,
    changed_rows,
):
    source = jnp.swapaxes(source_rows[0, 0], 0, 1)
    target = jnp.swapaxes(target_rows[0, 0], 0, 1)
    source_sums, target_sums = source_state[0], target_state[0]
    src, tgt, rel = source_ids[0, 0], target_ids[0, 0], relation_ids[0, 0]
    negatives, counts = negative_block[0, 0], edge_counts[0, 0]
    width, rows = source.shape
    shards = lax.axis_size("serve")
    matrix, line = ((width, rows), F32), ((1, rows), F32)
    edge16, edge32, grad16 = ((width, LIVE), BF16), ((width, LIVE), F32), ((rows, LIVE), BF16)
    shard, changed = serving_shard[0], changed_rows[0]
    payload, ids8 = ((width + TAIL, rows), jnp.int16), ((8, LIVE), jnp.int32)
    places = ((shards * 2 * SLOTS, rows), BF16)

    near_out = call(encode_target_kernel, [payload], (target,))[0]
    source_out, far_out, ids = call(
        encode_source_kernel, [payload, payload, ids8],
        (source, src, tgt, rel, negatives, counts, near_out, target_sums), (4, 5))
    near_target = from_behind(near_out, "dom", 1)
    near_source = from_behind(source_out, "dom", 1)
    far_target = from_behind(far_out, "dom", 2)
    q_high, q_low, relation, ids_next, top, bottom = call(
        query_kernel, [edge16, edge16, edge32, ids8, places, places],
        (source, relation_table, ids, src, tgt, rel, negatives, counts, shard, changed), (6, 7))
    source, source_sums, q_high, q_low, relation = call(
        source_kernel, [matrix, line, edge16, edge16, edge32],
        (near_target, source, source_sums, relation_table, ids, ids_next, q_high, q_low, relation), flops=8 * 10**9)
    far_target = lax.optimization_barrier((far_target, source_sums))[0]
    far_rows, far_state, far_parts = call(
        far_kernel, [matrix, line, ((rows, 3 * width), BF16)], (far_target,), flops=10**6)
    near_source = lax.optimization_barrier((near_source, far_state))[0]
    behind_high, behind_low, behind_ids = call(
        behind_kernel, [edge16, edge16, ids8], (near_source, relation_table), flops=10**6)
    source, source_sums, target, target_sums, g_high, g_low, outgoing = call(
        main_kernel, [matrix, line, matrix, line, grad16, grad16, ((shards, width // 2 + 8, 2 * SLOTS), BF16)],
        (far_rows, far_state, far_parts, behind_high, behind_low, behind_ids, source, source_sums, ids_next, q_high, q_low, relation, top, bottom))
    incoming = lax.all_to_all(outgoing, "serve", split_axis=0, concat_axis=0, tiled=True)
    target, target_sums, source, source_sums = call(
        last_target_kernel, [matrix, line, matrix, line],
        (target, target_sums, q_high, q_low, g_high, g_low, source, source_sums))
    served = pl.pallas_call(
        serve_kernel,
        out_shape=jax.ShapeDtypeStruct((shards, width, rows), BF16),
        in_specs=[VMEM],
        out_specs=pl.BlockSpec(memory_space=pl.ANY),
        scratch_shapes=[pltpu.VMEM((shards, width, rows), BF16), pltpu.SemaphoreType.DMA((shards,))],
        compiler_params=pltpu.CompilerParams(vmem_limit_bytes=40 * 2**20),
    )(incoming)
    return (
        jnp.swapaxes(source, 0, 1)[None, None],
        source_sums[None],
        jnp.swapaxes(target, 0, 1)[None, None],
        target_sums[None],
        jnp.swapaxes(served, 1, 2)[None, None],
    )


def solution(mesh):
    return jax.shard_map(
        on_device,
        mesh=mesh,
        in_specs=(
            P("dom", "serve", None, None),
            P("dom", "serve", None),
            P("dom", "serve", None, None),
            P("dom", "serve", None),
            P(),
            P("dom", "serve", None, None, None),
            P("dom", "serve", None, None, None),
            P("dom", "serve", None, None, None),
            P("dom", "serve", None, None),
            P("dom", "serve", None, None),
            P("dom", "serve", None),
            P("dom", "serve", None),
        ),
        out_specs=(
            P("dom", "serve", None, None),
            P("dom", "serve", None),
            P("dom", "serve", None, None),
            P("dom", "serve", None),
            P("dom", "serve", None, None, None),
        ),
        check_vma=False,
    )
```
